32 devices in a mesh: section: 4 (over x, core), dom: 8 (over z, y).
Axes of the slice: x: 2, y: 2, z: 4, core: 2. Of those that a mesh axis runs over, the one named last changes fastest.
Arguments:
- voltages: bfloat16 [512, 64, 2048], P('dom'), may hold values from -6 to 6
- station_map: int32 [512], replicated, may hold values from 0 to 511, each once
- beam_table: int32 [128, 512], replicated, may hold values from 0 to 63
- weight_table: bfloat16 [2, 64, 1024], P(None, None, 'dom'), may hold values from -0.3125 to 0.3125
- dm_trial: int32 [128], replicated, may hold values from 0 to 31
Outputs:
- power: float32 [128, 64, 1024], P(('section', 'dom'))
The draws below stay inside these ranges and needn't reach their ends.
Inputs may be any that keep to these rules, and one draw needn't show every extreme that they name: `station_map`: each of the 512 stations appears once.
All inputs are finite; a program needn't handle non-finite values.
Results may differ from the reference program's by a relative error of at most 0.0042.
Values may be sent and summed in bfloat16 or wider, within the bound.
A program may use at most 128 MiB of HBM per device.

```python
import math
import jax
import jax.numpy as jnp
from jax import lax

NSTAT = 512
NFFT = 2048
CH = 1024
BEAMS = 128
NTAB = 64
FRAMES = 64
NDM = 32


def place_ends(values, stream_key, smallest, largest):
    longest = values.shape.index(max(values.shape))
    spots = []
    for shift in (0, 1):
        where = [jax.random.randint(jax.random.fold_in(stream_key, axis), (), 0, length) for axis, length in enumerate(values.shape)]
        where[longest] = (where[longest] + shift) % values.shape[longest]
        spots.append(tuple(where))
    return values.at[spots[0]].set(smallest).at[spots[1]].set(largest)


def level_of(stream_key, dims, pieces, least, largest):
    factor_of, own = 1.0, jax.random.fold_in(stream_key, 6)
    for axis_at, blocks in pieces:
        heights = jnp.exp(jax.random.uniform(jax.random.fold_in(own, axis_at), (blocks,), jnp.float32, least / len(pieces), largest / len(pieces)))
        factor_of = factor_of * jnp.repeat(heights, dims[axis_at] // blocks).reshape([-1 if axis == axis_at else 1 for axis in range(len(dims))])
    return factor_of


def normal_values(rng, shape, scale, reach, cuts=(), kind=jnp.bfloat16):
    entries = scale * jax.random.normal(rng, shape, jnp.float32)
    if cuts:
        entries = entries * level_of(rng, shape, cuts, -0.22, 0.18)
    return jnp.clip(entries, -reach, reach).astype(kind)


def setup_inputs(seed: int = 0) -> dict:
    key_list = jax.random.split(jax.random.key(seed), 6)
    return {
        "voltages": normal_values(key_list[0], (NSTAT, FRAMES, NFFT), 1.0, 6.0, ((0, 8),)),
        "station_map": jax.random.permutation(key_list[1], NSTAT).astype(jnp.int32),
        "beam_table": place_ends(jax.random.randint(key_list[2], (BEAMS, NSTAT), 0, NTAB), jax.random.fold_in(key_list[2], 1), 0, NTAB - 1).astype(jnp.int32),
        "weight_table": normal_values(key_list[3], (2, NTAB, CH), (3 * NSTAT // 4) ** -0.5, 0.3125, ((2, 8),)),
        "dm_trial": place_ends(jax.random.randint(key_list[4], (BEAMS,), 0, NDM), jax.random.fold_in(key_list[4], 1), 0, NDM - 1).astype(jnp.int32),
    }


def dft_table():
    sample_index = jnp.arange(NFFT, dtype=jnp.int32)
    window = 0.5 - 0.5 * jnp.cos(sample_index.astype(jnp.float32) * (2.0 * math.pi / NFFT))
    column = jnp.arange(NFFT, dtype=jnp.int32)
    bin_index = column % CH
    product = sample_index[:, None] * bin_index[None, :] % NFFT
    angle = product.astype(jnp.float32) * (2.0 * math.pi / NFFT)
    values = jnp.where(column[None, :] < CH, jnp.cos(angle), -jnp.sin(angle))
    return (values * (window[:, None] / math.sqrt(NFFT))).astype(jnp.bfloat16)

def reference(voltages, station_map, beam_table, weight_table, dm_trial):
    table = dft_table()
    flat = voltages.reshape(NSTAT * FRAMES, NFFT)
    spectra = jnp.dot(flat, table, preferred_element_type=jnp.float32).reshape(NSTAT, FRAMES, NFFT)
    chan_re = spectra[:, :, :CH].astype(jnp.bfloat16)
    chan_im = spectra[:, :, CH:].astype(jnp.bfloat16)
    ordered = beam_table[:, station_map]
    block_size = min(64, CH)

    def form(block_index):
        start = (block_index * block_size).astype(jnp.int32)
        table_re = lax.dynamic_slice_in_dim(weight_table[0], start, block_size, 1)
        table_im = lax.dynamic_slice_in_dim(weight_table[1], start, block_size, 1)
        w_re = table_re[ordered].astype(jnp.float32)
        w_im = table_im[ordered].astype(jnp.float32)
        x_re = lax.dynamic_slice_in_dim(chan_re, start, block_size, 2).astype(jnp.float32)
        x_im = lax.dynamic_slice_in_dim(chan_im, start, block_size, 2).astype(jnp.float32)
        beam_re = jnp.einsum('bsc,sfc->bfc', w_re, x_re) - jnp.einsum('bsc,sfc->bfc', w_im, x_im)
        beam_im = jnp.einsum('bsc,sfc->bfc', w_re, x_im) + jnp.einsum('bsc,sfc->bfc', w_im, x_re)
        return (beam_re, beam_im)
    blocks_re, blocks_im = lax.map(form, jnp.arange(CH // block_size, dtype=jnp.int32))
    beams_re = jnp.transpose(blocks_re, (1, 2, 0, 3)).reshape(BEAMS, FRAMES, CH)
    beams_im = jnp.transpose(blocks_im, (1, 2, 0, 3)).reshape(BEAMS, FRAMES, CH)
    spectrum = jnp.fft.fft(beams_re + 1j * beams_im, axis=1)
    bins = jnp.arange(FRAMES, dtype=jnp.int32)
    kappa = jnp.where(bins < FRAMES // 2, bins, bins - FRAMES).astype(jnp.float32)
    freq = 1.0 + jnp.arange(CH, dtype=jnp.float32) / CH
    spread = 1.0 / (freq * freq * freq)
    measure = (dm_trial + 1).astype(jnp.float32) / NDM
    coeff = math.pi * measure[:, None] * spread[None, :]
    phase = coeff[:, None, :] * (kappa * kappa / FRAMES)[None, :, None]
    rotated = spectrum * (jnp.cos(phase) + 1j * jnp.sin(phase))
    series = jnp.fft.ifft(rotated, axis=1)
    power = jnp.real(series) * jnp.real(series) + jnp.imag(series) * jnp.imag(series)
    return power.astype(jnp.float32)
```

```python
import functools
import math

import jax
import jax.numpy as jnp
import ml_dtypes
import numpy as np
from jax import lax
from jax.experimental import pallas as pl
from jax.experimental.pallas import tpu as pltpu
from jax.sharding import PartitionSpec as P

NTAB = 64
NDM = 32
LANES = 128
TILE = 16
PAIR = 2
CHUNKS = 8
PASSES = 2
ROWS = 256
MESH = pl.DeviceIdType.MESH


def natural_channels(half, chunks):
    fine = half // (2 * chunks)
    chunk = np.arange(chunks)[:, None, None]
    side = np.arange(2)[None, :, None]
    return (side * (half // 2) + chunk * fine + np.arange(fine)[None, None, :]).reshape(chunks, 2 * fine)


def dft_rows(nfft, total, sections, chunks, passes):
    section = total // sections
    half = section // PAIR
    order = natural_channels(half, chunks).reshape(passes, -1)
    start = np.arange(sections)[:, None, None, None] * section
    chan = start + np.arange(PAIR)[None, None, :, None] * half + order[None, :, None, :]
    chan = chan.reshape(sections, passes, -1)
    sample = np.arange(nfft)
    window = (0.5 - 0.5 * np.cos(sample * (2.0 * math.pi / nfft))) / math.sqrt(nfft)
    angle = np.arange(nfft) * (2.0 * math.pi / nfft)
    cosine, sine = np.cos(angle), np.sin(angle)
    turn = chan[..., None] * sample % nfft
    rows = np.concatenate((cosine[turn] * window, -sine[turn] * window), axis=2)
    return rows.astype(np.float32).astype(ml_dtypes.bfloat16)


def split(values):
    values = values.astype(np.float32)
    high = values.astype(ml_dtypes.bfloat16)
    return high, (values - high.astype(np.float32)).astype(ml_dtypes.bfloat16)


def frame_matrices(frames):
    index = np.arange(frames)
    angle = (index[:, None] * index[None, :] % frames) * (2.0 * math.pi / frames)
    cosine, sine = np.cos(angle), np.sin(angle)
    real = np.concatenate((cosine, sine), axis=0)
    imag = np.concatenate((-sine, cosine), axis=0)
    forward = np.concatenate((real, imag, imag, real), axis=1)
    back_real = np.concatenate((cosine, -sine), axis=0)
    back_imag = np.concatenate((sine, cosine), axis=0)
    inverse = np.concatenate((back_real, back_imag), axis=1) / frames
    return split(forward) + split(inverse)


def pick_lanes(entries, where):
    dims = lax.GatherDimensionNumbers(
        offset_dims=(),
        collapsed_slice_dims=(1,),
        start_index_map=(1,),
        operand_batching_dims=(0,),
        start_indices_batching_dims=(0,),
    )
    return lax.gather(
        entries,
        where[..., None],
        dims,
        slice_sizes=(1, 1),
        mode=lax.GatherScatterMode.PROMISE_IN_BOUNDS,
    )


def dot(a, b):
    return jnp.dot(a, b, preferred_element_type=jnp.float32)


def cos_turns(turns):
    t = turns - jnp.round(turns)
    q = 0.25 - jnp.abs(t)
    x = q * q
    coeff = [(-1) ** k * (2.0 * math.pi) ** (2 * k + 1) / math.factorial(2 * k + 1) for k in range(7)]
    total = jnp.full_like(x, coeff[-1])
    for c in coeff[-2::-1]:
        total = total * x + c
    return total * q


def kernel(
    sections, doms, per, total,
    v_hbm, table_hbm, lut_ref, index_ref, meas_ref, fh_ref, fl_ref, gh_ref, gl_ref,
    out_ref,
    volts, table, lanes, ysend, x_buf, part, out_buf, in_right, in_left, sums, pw, rx, lut_rx, lut, where_ref,
    v_sem, t_sem, y_ss, y_rs, z_ss, zr_rs, zl_rs, p_ss, p_rs, l_ss, l_rs, l_sem,
):
    s = lax.axis_index("section")
    d = lax.axis_index("dom")
    z = d // PAIR
    y = d % PAIR
    line = doms // PAIR
    group = sections * PAIR
    me = s * PAIR + y
    stations = ysend.shape[2]
    frames = LANES // 2
    chunks, _, count, beams, _ = part.shape
    half = chunks * count
    chans = lut_ref.shape[0]
    blocks = half // chans
    fine = count // 2
    tiles = volts.shape[0] // ROWS
    held = x_buf.shape[1]

    def load(tile):
        span = pl.ds(pl.multiple_of(tile * ROWS, ROWS), ROWS)
        return pltpu.make_async_copy(v_hbm.at[span], volts.at[span], v_sem.at[tile])

    def load_table(step):
        return pltpu.make_async_copy(table_hbm.at[s, step], table.at[step], t_sem.at[step])

    load_table(0).start()
    lax.fori_loop(0, tiles, lambda t, c: (load(t).start(), c)[1], 0)
    for step in range(1, PASSES):
        load_table(step).start()

    def node(g):
        return (g // PAIR, z * PAIR + g % PAIR)

    target_s = d // (blocks * PAIR)
    target_y = d // blocks % PAIR
    block_slot = d % blocks
    home_z = z % sections

    def lut_target(m):
        return (target_s, (m * sections + s) * PAIR + target_y)

    def lut_to_self(m):
        dev = lut_target(m)
        return (dev[0] == s) & (dev[1] == d)

    def lut_source(q):
        return (home_z, me * blocks + q)

    def lut_from_self(q):
        dev = lut_source(q)
        return (dev[0] == s) & (dev[1] == d)

    def lut_copy(m):
        return pltpu.make_async_remote_copy(
            src_ref=lut_ref,
            dst_ref=lut_rx.at[block_slot],
            send_sem=l_ss.at[m],
            recv_sem=l_rs.at[block_slot],
            device_id=lut_target(m),
            device_id_type=MESH,
        )

    def lut_wait(q):
        return pltpu.make_async_remote_copy(
            src_ref=lut_ref,
            dst_ref=lut_rx.at[q],
            send_sem=l_ss.at[0],
            recv_sem=l_rs.at[q],
            device_id=(s, d),
            device_id_type=MESH,
        )

    barrier = pltpu.get_barrier_semaphore()
    for k in range(1, group):
        pl.semaphore_signal(barrier, 1, device_id=node((me + k) % group), device_id_type=MESH)

    @pl.when(z > 0)
    def _():
        pl.semaphore_signal(barrier, 1, device_id=(s, d - PAIR), device_id_type=MESH)

    @pl.when(z < line - 1)
    def _():
        pl.semaphore_signal(barrier, 1, device_id=(s, d + PAIR), device_id_type=MESH)

    for q in range(blocks):

        @pl.when(jnp.logical_not(lut_from_self(q)))
        def _():
            pl.semaphore_signal(barrier, 1, device_id=lut_source(q), device_id_type=MESH)

    arrivals = group - 1 + (z > 0).astype(jnp.int32) + (z < line - 1).astype(jnp.int32)
    for m in range(blocks):
        arrivals = arrivals + jnp.logical_not(lut_to_self(m)).astype(jnp.int32)
    pl.semaphore_wait(barrier, arrivals)

    for m in range(blocks):

        @pl.when(jnp.logical_not(lut_to_self(m)))
        def _():
            lut_copy(m).start()

        @pl.when(lut_to_self(m))
        def _():
            own = pltpu.make_async_copy(lut_ref, lut_rx.at[block_slot], l_sem)
            own.start()
            own.wait()

    for part_at in range(2):
        where_ref[part_at] = (index_ref[...] + part_at * NTAB).astype(jnp.int16)

    first_half = lax.broadcasted_iota(jnp.int32, (1, LANES), 1) < frames
    half_rows = half // PASSES * PAIR
    chunk_pass = chunks // PASSES

    def y_copy(j):
        return pltpu.make_async_remote_copy(
            src_ref=ysend.at[j],
            dst_ref=x_buf.at[pl.ds(j * count, count), pl.ds(pl.multiple_of(y * stations, TILE), stations)],
            send_sem=y_ss.at[j],
            recv_sem=y_rs.at[j],
            device_id=(s, z * PAIR + 1 - y),
            device_id_type=MESH,
        )

    def channelise(step):
        load_table(step).wait()

        def tile_body(tile, carry):
            if step == 0:
                load(tile).wait()
            span = pl.ds(pl.multiple_of(tile * ROWS, ROWS), ROWS)
            o = lax.dot_general(
                table[step], volts[span], (((1,), (1,)), ((), ())), preferred_element_type=jnp.float32
            )
            for two in range(ROWS // LANES):
                a = o[:half_rows, two * LANES : (two + 1) * LANES]
                b = o[half_rows:, two * LANES : (two + 1) * LANES]
                even = jnp.where(first_half, a, pltpu.roll(b, frames, 1))
                odd = jnp.where(first_half, pltpu.roll(a, frames, 1), b)
                row = tile * (ROWS // frames) + two * 2
                lanes[pl.ds(row, half_rows, stride=stations), :] = even
                lanes[pl.ds(row + 1, half_rows, stride=stations), :] = odd
            return carry

        lax.fori_loop(0, tiles, tile_body, 0)
        size = count * stations

        def send_body(jj, carry):
            j = jj + step * chunk_pass
            start = pl.multiple_of(((1 - y) * chunk_pass + jj) * size, size)
            ysend[j] = lanes[pl.ds(start, size), :].astype(jnp.bfloat16).reshape(count, stations, LANES)
            y_copy(j).start()
            return carry

        lax.fori_loop(0, chunk_pass, send_body, 0)

        def keep_body(jj, carry):
            j = jj + step * chunk_pass
            start = pl.multiple_of((y * chunk_pass + jj) * size, size)
            mine = lanes[pl.ds(start, size), :].astype(jnp.bfloat16).reshape(count, stations, LANES)
            x_buf[pl.ds(j * count, count), pl.ds(pl.multiple_of(y * stations, TILE), stations)] = mine
            return carry

        lax.fori_loop(0, chunk_pass, keep_body, 0)

    sign = jnp.where(first_half, -1.0, 1.0)

    def form(j):
        y_copy(j).wait_recv()

        def chan_body(fc, carry):
            for side in range(2):
                row = side * (half // 2) + j * fine + fc
                entry = jnp.broadcast_to(lut[pl.ds(row, 1), :].astype(jnp.bfloat16), (TILE, LANES))
                weights = jnp.concatenate(
                    [
                        pick_lanes(entry, where_ref[p, t * TILE : (t + 1) * TILE, :])
                        for p in range(2)
                        for t in range(where_ref.shape[1] // TILE)
                    ],
                    axis=0,
                )
                cc = side * fine + fc
                product = dot(weights[:, :held], x_buf[j * count + cc])
                all_beams = where_ref.shape[1]
                beam = product[:all_beams] + sign * pltpu.roll(product[all_beams:], frames, 1)
                for to in range(line):
                    part[j, to, cc] = beam[to * beams : (to + 1) * beams]
            return carry

        lax.fori_loop(0, fine, chan_body, 0)

    def right_copy(j, to):
        return pltpu.make_async_remote_copy(
            src_ref=out_buf.at[j, to],
            dst_ref=in_right.at[j, to],
            send_sem=z_ss.at[j, to],
            recv_sem=zr_rs.at[j, to],
            device_id=(s, jnp.minimum(d + PAIR, doms - PAIR + y)),
            device_id_type=MESH,
        )

    def left_copy(j, to):
        return pltpu.make_async_remote_copy(
            src_ref=out_buf.at[j, to],
            dst_ref=in_left.at[j, to],
            send_sem=z_ss.at[j, to],
            recv_sem=zl_rs.at[j, to],
            device_id=(s, jnp.maximum(d - PAIR, y)),
            device_id_type=MESH,
        )

    def begin(j):
        for to in range(line - 1, 0, -1):

            @pl.when(z == 0)
            def _():
                out_buf[j, to] = part[j, to].astype(jnp.bfloat16)
                right_copy(j, to).start()

        for to in range(line - 1):

            @pl.when(z == line - 1)
            def _():
                out_buf[j, to] = part[j, to].astype(jnp.bfloat16)
                left_copy(j, to).start()

    def relay(j):
        for to in range(line - 1, 0, -1):

            @pl.when((z > 0) & (z < to))
            def _():
                right_copy(j, to).wait_recv()
                out_buf[j, to] = (part[j, to] + in_right[j, to].astype(jnp.float32)).astype(jnp.bfloat16)
                right_copy(j, to).start()

        for to in range(line - 1):

            @pl.when((z < line - 1) & (z > to))
            def _():
                left_copy(j, to).wait_recv()
                out_buf[j, to] = (part[j, to] + in_left[j, to].astype(jnp.float32)).astype(jnp.bfloat16)
                left_copy(j, to).start()

    def power_copy(j, k):
        g = (me + k) % group
        return pltpu.make_async_remote_copy(
            src_ref=pw.at[j, g],
            dst_ref=rx.at[me, j],
            send_sem=p_ss.at[j, k],
            recv_sem=p_rs.at[j, k],
            device_id=node(g),
            device_id_type=MESH,
        )

    lane = lax.broadcasted_iota(jnp.int32, (1, LANES), 1)
    bins = lane % frames
    kappa = jnp.where(bins < frames // 2, bins, bins - frames).astype(jnp.float32)
    turn_rate = kappa * kappa * (0.5 / frames)
    quarter = jnp.where(first_half, 0.0, 0.25)

    def finish(j):
        sums[...] = part[j, z].reshape(count * beams, LANES)

        @pl.when(z > 0)
        def _():
            right_copy(j, z).wait_recv()
            sums[...] += in_right[j, z].astype(jnp.float32).reshape(count * beams, LANES)

        @pl.when(z < line - 1)
        def _():
            left_copy(j, z).wait_recv()
            sums[...] += in_left[j, z].astype(jnp.float32).reshape(count * beams, LANES)

        within = lax.broadcasted_iota(jnp.int32, (count, LANES), 0)
        chan = me * half + within // fine * (half // 2) + j * fine + within % fine
        freq = 1.0 + chan.astype(jnp.float32) * (1.0 / total)
        rate = turn_rate / (freq * freq * freq)
        rows = [sums[pl.ds(b, count, stride=beams), :] for b in range(beams)]
        x = jnp.concatenate(rows, axis=0)
        high = x.astype(jnp.bfloat16)
        low = (x - high.astype(jnp.float32)).astype(jnp.bfloat16)
        spec = dot(high, fh_ref[...]) + dot(low, fh_ref[...]) + dot(high, fl_ref[...])
        turns = jnp.concatenate([meas_ref[b : b + 1, :] * rate - quarter for b in range(beams)], axis=0)
        chirp = cos_turns(turns)
        other = pltpu.roll(chirp, frames, 1)
        cosine = jnp.where(first_half, chirp, other)
        sine = jnp.where(first_half, -other, chirp)
        turned = spec[:, :LANES] * cosine + spec[:, LANES:] * sine
        high = turned.astype(jnp.bfloat16)
        low = (turned - high.astype(jnp.float32)).astype(jnp.bfloat16)
        series = dot(high, gh_ref[...]) + dot(low, gh_ref[...]) + dot(high, gl_ref[...])
        square = series * series
        power = square + pltpu.roll(square, frames, 1)
        power = power.reshape(beams, 2, fine, LANES)
        packed = jnp.where(first_half[None], power[:, 0], power[:, 1])
        pw[j] = packed.reshape(group, per * fine, LANES)
        for k in range(1, group):
            power_copy(j, k).start()
        rx[me, j] = pw[j, me]

    channelise(0)
    for q in range(blocks):

        @pl.when(jnp.logical_not(lut_from_self(q)))
        def _():
            lut_wait(q).wait_recv()

    lut[...] = lut_rx[...].astype(jnp.float32).reshape(half, LANES)

    early = chunk_pass // 2
    late = 2

    def step_body(i, carry):
        @pl.when(i < chunks)
        def _():
            form(i)
            begin(i)

        @pl.when((i >= 1) & (i <= chunks))
        def _():
            relay(i - 1)

        @pl.when(i >= late)
        def _():
            finish(i - late)

        return carry

    lax.fori_loop(0, early, step_body, 0)
    channelise(1)
    lax.fori_loop(early, chunks + late, step_body, 0)

    def drain(j, carry):
        y_copy(j).wait_send()
        for to in range(line):

            @pl.when(z < to)
            def _():
                right_copy(j, to).wait_send()

            @pl.when(z > to)
            def _():
                left_copy(j, to).wait_send()

        for k in range(1, group):
            power_copy(j, k).wait()
        return carry

    lax.fori_loop(0, chunks, drain, 0)
    for m in range(blocks):

        @pl.when(jnp.logical_not(lut_to_self(m)))
        def _():
            lut_copy(m).wait_send()

    def out_body(g, carry):
        for b in range(per):
            block = rx[g, :, b * fine : (b + 1) * fine, :].reshape(half // 2, LANES).T
            out_ref[b, :, pl.ds(pl.multiple_of(g * half, half), half)] = jnp.concatenate(
                (block[:frames], block[frames:]), axis=1
            )
        return carry

    lax.fori_loop(0, group, out_body, 0)


def body(voltages, station_map, beam_table, weight_table, dm_trial):
    sections = lax.axis_size("section")
    doms = lax.axis_size("dom")
    z = lax.axis_index("dom") // PAIR
    stations, frames, nfft = voltages.shape
    beams = beam_table.shape[0]
    chans = weight_table.shape[2]
    total = chans * doms
    line = doms // PAIR
    group = sections * PAIR
    per = beams // (sections * doms)
    half = total // group
    here = beams // line
    count = half // CHUNKS
    held = PAIR * stations

    table = dft_rows(nfft, total, sections, CHUNKS, PASSES)
    matrices = frame_matrices(frames)
    lut = weight_table.transpose(2, 0, 1).reshape(chans, 2 * NTAB)
    mine = lax.dynamic_slice_in_dim(station_map, z * held, held, 0)
    ordered = beam_table.reshape(sections, line, PAIR * per, -1).transpose(1, 0, 2, 3).reshape(beams, -1)
    index = jnp.take(ordered, mine, axis=1, mode="clip")
    index = jnp.pad(index, ((0, 0), (0, LANES - held)))
    trials = dm_trial.reshape(sections, line, PAIR * per)
    trials = lax.dynamic_slice_in_dim(trials, z, 1, 1).reshape(here, 1)
    measure = jnp.broadcast_to((trials + 1).astype(jnp.float32) / NDM, (here, LANES))

    vmem = pl.BlockSpec(memory_space=pltpu.VMEM)
    hbm = pl.BlockSpec(memory_space=pl.ANY)
    dma = pltpu.SemaphoreType.DMA
    bf16, f32 = jnp.bfloat16, jnp.float32
    return pl.pallas_call(
        functools.partial(kernel, sections, doms, per, total),
        in_specs=[hbm, hbm] + [vmem] * 7,
        out_specs=vmem,
        out_shape=jax.ShapeDtypeStruct((per, frames, total), f32),
        scratch_shapes=[
            pltpu.VMEM((stations * frames, nfft), bf16),
            pltpu.VMEM(table.shape[1:], bf16),
            pltpu.VMEM((PAIR * half // PASSES * stations, LANES), f32),
            pltpu.VMEM((CHUNKS, count, stations, LANES), bf16),
            pltpu.VMEM((half, held, LANES), bf16),
            pltpu.VMEM((CHUNKS, line, count, here, LANES), f32),
            pltpu.VMEM((CHUNKS, line, count, here, LANES), bf16),
            pltpu.VMEM((CHUNKS, line, count, here, LANES), bf16),
            pltpu.VMEM((CHUNKS, line, count, here, LANES), bf16),
            pltpu.VMEM((count * here, LANES), f32),
            pltpu.VMEM((CHUNKS, group, per * count // 2, LANES), f32),
            pltpu.VMEM((group, CHUNKS, per * count // 2, LANES), f32),
            pltpu.VMEM((half // chans, chans, LANES), bf16),
            pltpu.VMEM((half, LANES), f32),
            pltpu.VMEM((2, beams, LANES), jnp.int16),
            dma((stations * frames // ROWS,)),
            dma((PASSES,)),
            dma((CHUNKS,)),
            dma((CHUNKS,)),
            dma((CHUNKS, line)),
            dma((CHUNKS, line)),
            dma((CHUNKS, line)),
            dma((CHUNKS, group)),
            dma((CHUNKS, group)),
            dma((half // chans,)),
            dma((half // chans,)),
            dma,
        ],
        compiler_params=pltpu.CompilerParams(
            collective_id=0, has_side_effects=True, vmem_limit_bytes=60 << 20
        ),
        cost_estimate=pl.CostEstimate(
            flops=2 * stations * frames * nfft * 2 * total // sections,
            bytes_accessed=2 * stations * frames * nfft,
            transcendentals=0,
        ),
        name="beamformer",
    )(
        voltages.reshape(stations * frames, nfft),
        jnp.asarray(table),
        lut,
        index,
        measure,
        *(jnp.asarray(m) for m in matrices),
    )


def solution(mesh):
    in_specs = (P("dom", None, None), P(), P(), P(None, None, "dom"), P())
    out_specs = P(("section", "dom"), None, None)
    return jax.shard_map(body, mesh=mesh, in_specs=in_specs, out_specs=out_specs, check_vma=False)
```

```python
import functools
import math

import jax
import jax.numpy as jnp
import ml_dtypes
import numpy as np
from jax import lax
from jax.experimental import pallas as pl
from jax.experimental.pallas import tpu as pltpu
from jax.sharding import PartitionSpec as P

NTAB = 64
NDM = 32
LANES = 128
TILE = 16
PAIR = 2
CHUNKS = 8
PASSES = 2
ROWS = 256
PAD = 8
MESH = pl.DeviceIdType.MESH


def natural_channels(half, chunks):
    fine = half // (2 * chunks)
    chunk = np.arange(chunks)[:, None, None]
    side = np.arange(2)[None, :, None]
    return (side * (half // 2) + chunk * fine + np.arange(fine)[None, None, :]).reshape(chunks, 2 * fine)


def dft_rows(nfft, total, sections, chunks, passes):
    section = total // sections
    half = section // PAIR
    order = natural_channels(half, chunks).reshape(passes, -1)
    start = np.arange(sections)[:, None, None, None] * section
    chan = start + np.arange(PAIR)[None, None, :, None] * half + order[None, :, None, :]
    chan = chan.reshape(sections, passes, -1)
    sample = np.arange(nfft)
    window = (0.5 - 0.5 * np.cos(sample * (2.0 * math.pi / nfft))) / math.sqrt(nfft)
    angle = np.arange(nfft) * (2.0 * math.pi / nfft)
    cosine, sine = np.cos(angle), np.sin(angle)
    turn = chan[..., None] * sample % nfft
    rows = np.concatenate((cosine[turn] * window, -sine[turn] * window), axis=2)
    return rows.astype(np.float32).astype(ml_dtypes.bfloat16)


def split(values):
    values = values.astype(np.float32)
    high = values.astype(ml_dtypes.bfloat16)
    return high, (values - high.astype(np.float32)).astype(ml_dtypes.bfloat16)


def frame_matrices(frames):
    index = np.arange(frames)
    angle = (index[:, None] * index[None, :] % frames) * (2.0 * math.pi / frames)
    cosine, sine = np.cos(angle), np.sin(angle)
    real = np.concatenate((cosine, sine), axis=0)
    imag = np.concatenate((-sine, cosine), axis=0)
    forward = np.concatenate((real, imag, imag, real), axis=1)
    back_real = np.concatenate((cosine, -sine), axis=0)
    back_imag = np.concatenate((sine, cosine), axis=0)
    inverse = np.concatenate((back_real, back_imag), axis=1) / frames
    return split(forward) + split(inverse)


def pick_lanes(entries, where):
    dims = lax.GatherDimensionNumbers(
        offset_dims=(),
        collapsed_slice_dims=(1,),
        start_index_map=(1,),
        operand_batching_dims=(0,),
        start_indices_batching_dims=(0,),
    )
    return lax.gather(
        entries,
        where[..., None],
        dims,
        slice_sizes=(1, 1),
        mode=lax.GatherScatterMode.PROMISE_IN_BOUNDS,
    )


def dot(a, b):
    return jnp.dot(a, b, preferred_element_type=jnp.float32)


def cos_turns(turns):
    t = turns - jnp.round(turns)
    q = 0.25 - jnp.abs(t)
    x = q * q
    coeff = [(-1) ** k * (2.0 * math.pi) ** (2 * k + 1) / math.factorial(2 * k + 1) for k in range(7)]
    total = jnp.full_like(x, coeff[-1])
    for c in coeff[-2::-1]:
        total = total * x + c
    return total * q


def kernel(
    sections, doms, per, total,
    v_hbm, table_hbm, lut_ref, index_ref, meas_ref, fh_ref, fl_ref, gh_ref, gl_ref,
    out_ref,
    volts, table, lanes, ysend, x_buf, part, out_buf, in_right, in_left, sums, pw, rx, lut_rx, lut, where_ref,
    v_sem, t_sem, y_ss, y_rs, z_ss, zr_rs, zl_rs, p_ss, p_rs, l_ss, l_rs, l_sem,
):
    s = lax.axis_index("section")
    d = lax.axis_index("dom")
    z = d // PAIR
    y = d % PAIR
    line = doms // PAIR
    group = sections * PAIR
    me = s * PAIR + y
    stations = ysend.shape[2]
    frames = LANES // 2
    chunks, _, count, beams, _ = part.shape
    half = chunks * count
    chans = lut_ref.shape[0]
    blocks = half // chans
    fine = count // 2
    tiles = volts.shape[0] // ROWS
    held = x_buf.shape[1]

    def load(tile):
        span = pl.ds(pl.multiple_of(tile * ROWS, ROWS), ROWS)
        return pltpu.make_async_copy(v_hbm.at[span], volts.at[span], v_sem.at[tile])

    def load_table(step):
        return pltpu.make_async_copy(table_hbm.at[s, step], table.at[step], t_sem.at[step])

    load_table(0).start()
    lax.fori_loop(0, tiles, lambda t, c: (load(t).start(), c)[1], 0)
    for step in range(1, PASSES):
        load_table(step).start()

    def node(g):
        return (g // PAIR, z * PAIR + g % PAIR)

    target_s = d // (blocks * PAIR)
    target_y = d // blocks % PAIR
    block_slot = d % blocks
    home_z = z % sections

    def lut_target(m):
        return (target_s, (m * sections + s) * PAIR + target_y)

    def lut_to_self(m):
        dev = lut_target(m)
        return (dev[0] == s) & (dev[1] == d)

    def lut_source(q):
        return (home_z, me * blocks + q)

    def lut_from_self(q):
        dev = lut_source(q)
        return (dev[0] == s) & (dev[1] == d)

    def lut_copy(m):
        return pltpu.make_async_remote_copy(
            src_ref=lut_ref,
            dst_ref=lut_rx.at[block_slot],
            send_sem=l_ss.at[m],
            recv_sem=l_rs.at[block_slot],
            device_id=lut_target(m),
            device_id_type=MESH,
        )

    def lut_wait(q):
        return pltpu.make_async_remote_copy(
            src_ref=lut_ref,
            dst_ref=lut_rx.at[q],
            send_sem=l_ss.at[0],
            recv_sem=l_rs.at[q],
            device_id=(s, d),
            device_id_type=MESH,
        )

    barrier = pltpu.get_barrier_semaphore()
    for k in range(1, group):
        pl.semaphore_signal(barrier, 1, device_id=node((me + k) % group), device_id_type=MESH)

    @pl.when(z > 0)
    def _():
        pl.semaphore_signal(barrier, 1, device_id=(s, d - PAIR), device_id_type=MESH)

    @pl.when(z < line - 1)
    def _():
        pl.semaphore_signal(barrier, 1, device_id=(s, d + PAIR), device_id_type=MESH)

    for q in range(blocks):

        @pl.when(jnp.logical_not(lut_from_self(q)))
        def _():
            pl.semaphore_signal(barrier, 1, device_id=lut_source(q), device_id_type=MESH)

    arrivals = group - 1 + (z > 0).astype(jnp.int32) + (z < line - 1).astype(jnp.int32)
    for m in range(blocks):
        arrivals = arrivals + jnp.logical_not(lut_to_self(m)).astype(jnp.int32)
    pl.semaphore_wait(barrier, arrivals)

    for m in range(blocks):

        @pl.when(jnp.logical_not(lut_to_self(m)))
        def _():
            lut_copy(m).start()

        @pl.when(lut_to_self(m))
        def _():
            own = pltpu.make_async_copy(lut_ref, lut_rx.at[block_slot], l_sem)
            own.start()
            own.wait()

    for part_at in range(2):
        where_ref[part_at] = (index_ref[...] + part_at * NTAB).astype(jnp.int16)

    first_half = lax.broadcasted_iota(jnp.int32, (1, LANES), 1) < frames
    half_rows = half // PASSES * PAIR
    pitch = lanes.shape[0] // half_rows
    chunk_pass = chunks // PASSES

    def y_copy(j):
        return pltpu.make_async_remote_copy(
            src_ref=ysend.at[j],
            dst_ref=x_buf.at[pl.ds(j * count, count), pl.ds(pl.multiple_of(y * stations, TILE), stations)],
            send_sem=y_ss.at[j],
            recv_sem=y_rs.at[j],
            device_id=(s, z * PAIR + 1 - y),
            device_id_type=MESH,
        )

    def channelise(step):
        load_table(step).wait()

        def tile_body(tile, carry):
            if step == 0:
                load(tile).wait()
            span = pl.ds(pl.multiple_of(tile * ROWS, ROWS), ROWS)
            o = lax.dot_general(
                table[step], volts[span], (((1,), (1,)), ((), ())), preferred_element_type=jnp.float32
            )
            for two in range(ROWS // LANES):
                a = o[:half_rows, two * LANES : (two + 1) * LANES]
                b = o[half_rows:, two * LANES : (two + 1) * LANES]
                even = jnp.where(first_half, a, pltpu.roll(b, frames, 1))
                odd = jnp.where(first_half, pltpu.roll(a, frames, 1), b)
                row = tile * (ROWS // frames) + two * 2
                lanes[pl.ds(row, half_rows, stride=pitch), :] = even
                lanes[pl.ds(row + 1, half_rows, stride=pitch), :] = odd
            return carry

        lax.fori_loop(0, tiles, tile_body, 0)

        def spectra(of, jj, cc):
            row = ((of * chunk_pass + jj) * count + cc) * pitch
            return lanes[pl.ds(row, stations), :].astype(jnp.bfloat16)

        def send_body(jj, carry):
            j = jj + step * chunk_pass
            for cc in range(count):
                ysend[j, cc] = spectra(1 - y, jj, cc)
            y_copy(j).start()
            return carry

        lax.fori_loop(0, chunk_pass, send_body, 0)

        def keep_body(jj, carry):
            j = jj + step * chunk_pass
            for cc in range(count):
                x_buf[j * count + cc, pl.ds(pl.multiple_of(y * stations, TILE), stations)] = spectra(y, jj, cc)
            return carry

        lax.fori_loop(0, chunk_pass, keep_body, 0)

    sign = jnp.where(first_half, -1.0, 1.0)

    def form(j):
        y_copy(j).wait_recv()

        def chan_body(fc, carry):
            for side in range(2):
                row = side * (half // 2) + j * fine + fc
                entry = jnp.broadcast_to(lut[pl.ds(row, 1), :].astype(jnp.bfloat16), (TILE, LANES))
                weights = jnp.concatenate(
                    [
                        pick_lanes(entry, where_ref[p, t * TILE : (t + 1) * TILE, :])
                        for p in range(2)
                        for t in range(where_ref.shape[1] // TILE)
                    ],
                    axis=0,
                )
                cc = side * fine + fc
                product = dot(weights[:, :held], x_buf[j * count + cc])
                all_beams = where_ref.shape[1]
                beam = product[:all_beams] + sign * pltpu.roll(product[all_beams:], frames, 1)
                for to in range(line):
                    part[j, to, cc] = beam[to * beams : (to + 1) * beams]
            return carry

        lax.fori_loop(0, fine, chan_body, 0, unroll=4)

    def right_copy(j, to):
        return pltpu.make_async_remote_copy(
            src_ref=out_buf.at[j, to],
            dst_ref=in_right.at[j, to],
            send_sem=z_ss.at[j, to],
            recv_sem=zr_rs.at[j, to],
            device_id=(s, jnp.minimum(d + PAIR, doms - PAIR + y)),
            device_id_type=MESH,
        )

    def left_copy(j, to):
        return pltpu.make_async_remote_copy(
            src_ref=out_buf.at[j, to],
            dst_ref=in_left.at[j, to],
            send_sem=z_ss.at[j, to],
            recv_sem=zl_rs.at[j, to],
            device_id=(s, jnp.maximum(d - PAIR, y)),
            device_id_type=MESH,
        )

    def begin(j):
        for to in range(line - 1, 0, -1):

            @pl.when(z == 0)
            def _():
                out_buf[j, to] = part[j, to].astype(jnp.bfloat16)
                right_copy(j, to).start()

        for to in range(line - 1):

            @pl.when(z == line - 1)
            def _():
                out_buf[j, to] = part[j, to].astype(jnp.bfloat16)
                left_copy(j, to).start()

    def relay_right(j):
        for to in range(line - 1, 0, -1):

            @pl.when(z < to)
            def _():
                right_copy(j, to).wait_recv()
                out_buf[j, to] = (part[j, to] + in_right[j, to].astype(jnp.float32)).astype(jnp.bfloat16)
                right_copy(j, to).start()

    def relay_left(j):
        for to in range(line - 1):

            @pl.when(z > to)
            def _():
                left_copy(j, to).wait_recv()
                out_buf[j, to] = (part[j, to] + in_left[j, to].astype(jnp.float32)).astype(jnp.bfloat16)
                left_copy(j, to).start()

    def power_copy(j, k):
        g = (me + k) % group
        return pltpu.make_async_remote_copy(
            src_ref=pw.at[j, g],
            dst_ref=rx.at[me, j],
            send_sem=p_ss.at[j, k],
            recv_sem=p_rs.at[j, k],
            device_id=node(g),
            device_id_type=MESH,
        )

    lane = lax.broadcasted_iota(jnp.int32, (1, LANES), 1)
    bins = lane % frames
    kappa = jnp.where(bins < frames // 2, bins, bins - frames).astype(jnp.float32)
    turn_rate = kappa * kappa * (0.5 / frames)
    quarter = jnp.where(first_half, 0.0, 0.25)

    def finish(j):
        sums[...] = part[j, z].reshape(count * beams, LANES)

        @pl.when(z > 0)
        def _():
            right_copy(j, z).wait_recv()
            sums[...] += in_right[j, z].astype(jnp.float32).reshape(count * beams, LANES)

        @pl.when(z < line - 1)
        def _():
            left_copy(j, z).wait_recv()
            sums[...] += in_left[j, z].astype(jnp.float32).reshape(count * beams, LANES)

        within = lax.broadcasted_iota(jnp.int32, (count, LANES), 0)
        chan = me * half + within // fine * (half // 2) + j * fine + within % fine
        freq = 1.0 + chan.astype(jnp.float32) * (1.0 / total)
        rate = turn_rate / (freq * freq * freq)
        rows = [sums[pl.ds(b, count, stride=beams), :] for b in range(beams)]
        x = jnp.concatenate(rows, axis=0)
        high = x.astype(jnp.bfloat16)
        low = (x - high.astype(jnp.float32)).astype(jnp.bfloat16)
        spec = dot(high, fh_ref[...]) + dot(low, fh_ref[...]) + dot(high, fl_ref[...])
        turns = jnp.concatenate([meas_ref[b : b + 1, :] * rate - quarter for b in range(beams)], axis=0)
        chirp = cos_turns(turns)
        other = pltpu.roll(chirp, frames, 1)
        cosine = jnp.where(first_half, chirp, other)
        sine = jnp.where(first_half, -other, chirp)
        turned = spec[:, :LANES] * cosine + spec[:, LANES:] * sine
        high = turned.astype(jnp.bfloat16)
        low = (turned - high.astype(jnp.float32)).astype(jnp.bfloat16)
        series = dot(high, gh_ref[...]) + dot(low, gh_ref[...]) + dot(high, gl_ref[...])
        square = series * series
        power = square + pltpu.roll(square, frames, 1)
        power = power.reshape(beams, 2, fine, LANES)
        packed = jnp.where(first_half[None], power[:, 0], power[:, 1])
        pw[j] = packed.reshape(group, per * fine, LANES)
        for k in range(1, group):
            power_copy(j, k).start()
        rx[me, j] = pw[j, me]

    channelise(0)
    for q in range(blocks):

        @pl.when(jnp.logical_not(lut_from_self(q)))
        def _():
            lut_wait(q).wait_recv()

    lut[...] = lut_rx[...].astype(jnp.float32).reshape(half, LANES)

    early = chunk_pass // 2
    late = line

    def step_body(i, carry):
        @pl.when(i < chunks)
        def _():
            form(i)
            begin(i)

        right_at = i - z
        left_at = i - (line - 1 - z)

        @pl.when((z > 0) & (right_at >= 0) & (right_at < chunks))
        def _():
            relay_right(right_at)

        @pl.when((z < line - 1) & (left_at >= 0) & (left_at < chunks))
        def _():
            relay_left(left_at)

        @pl.when(i >= late)
        def _():
            finish(i - late)

        return carry

    lax.fori_loop(0, early, step_body, 0)
    channelise(1)
    lax.fori_loop(early, chunks + late, step_body, 0)

    def drain(j, carry):
        y_copy(j).wait_send()
        for to in range(line):

            @pl.when(z < to)
            def _():
                right_copy(j, to).wait_send()

            @pl.when(z > to)
            def _():
                left_copy(j, to).wait_send()

        for k in range(1, group):
            power_copy(j, k).wait()
        return carry

    lax.fori_loop(0, chunks, drain, 0)
    for m in range(blocks):

        @pl.when(jnp.logical_not(lut_to_self(m)))
        def _():
            lut_copy(m).wait_send()

    def out_body(g, carry):
        for b in range(per):
            block = rx[g, :, b * fine : (b + 1) * fine, :].reshape(half // 2, LANES).T
            out_ref[b, :, pl.ds(pl.multiple_of(g * half, half), half)] = jnp.concatenate(
                (block[:frames], block[frames:]), axis=1
            )
        return carry

    lax.fori_loop(0, group, out_body, 0)


def body(voltages, station_map, beam_table, weight_table, dm_trial):
    sections = lax.axis_size("section")
    doms = lax.axis_size("dom")
    z = lax.axis_index("dom") // PAIR
    stations, frames, nfft = voltages.shape
    beams = beam_table.shape[0]
    chans = weight_table.shape[2]
    total = chans * doms
    line = doms // PAIR
    group = sections * PAIR
    per = beams // (sections * doms)
    half = total // group
    here = beams // line
    count = half // CHUNKS
    held = PAIR * stations

    table = dft_rows(nfft, total, sections, CHUNKS, PASSES)
    matrices = frame_matrices(frames)
    lut = weight_table.transpose(2, 0, 1).reshape(chans, 2 * NTAB)
    mine = lax.dynamic_slice_in_dim(station_map, z * held, held, 0)
    ordered = beam_table.reshape(sections, line, PAIR * per, -1).transpose(1, 0, 2, 3).reshape(beams, -1)
    index = jnp.take(ordered, mine, axis=1, mode="clip")
    index = jnp.pad(index, ((0, 0), (0, LANES - held)))
    trials = dm_trial.reshape(sections, line, PAIR * per)
    trials = lax.dynamic_slice_in_dim(trials, z, 1, 1).reshape(here, 1)
    measure = jnp.broadcast_to((trials + 1).astype(jnp.float32) / NDM, (here, LANES))

    vmem = pl.BlockSpec(memory_space=pltpu.VMEM)
    hbm = pl.BlockSpec(memory_space=pl.ANY)
    dma = pltpu.SemaphoreType.DMA
    bf16, f32 = jnp.bfloat16, jnp.float32
    return pl.pallas_call(
        functools.partial(kernel, sections, doms, per, total),
        in_specs=[hbm, hbm] + [vmem] * 7,
        out_specs=vmem,
        out_shape=jax.ShapeDtypeStruct((per, frames, total), f32),
        scratch_shapes=[
            pltpu.VMEM((stations * frames, nfft), bf16),
            pltpu.VMEM(table.shape[1:], bf16),
            pltpu.VMEM((PAIR * half // PASSES * (stations + PAD), LANES), f32),
            pltpu.VMEM((CHUNKS, count, stations, LANES), bf16),
            pltpu.VMEM((half, held, LANES), bf16),
            pltpu.VMEM((CHUNKS, line, count, here, LANES), f32),
            pltpu.VMEM((CHUNKS, line, count, here, LANES), bf16),
            pltpu.VMEM((CHUNKS, line, count, here, LANES), bf16),
            pltpu.VMEM((CHUNKS, line, count, here, LANES), bf16),
            pltpu.VMEM((count * here, LANES), f32),
            pltpu.VMEM((CHUNKS, group, per * count // 2, LANES), f32),
            pltpu.VMEM((group, CHUNKS, per * count // 2, LANES), f32),
            pltpu.VMEM((half // chans, chans, LANES), bf16),
            pltpu.VMEM((half, LANES), f32),
            pltpu.VMEM((2, beams, LANES), jnp.int16),
            dma((stations * frames // ROWS,)),
            dma((PASSES,)),
            dma((CHUNKS,)),
            dma((CHUNKS,)),
            dma((CHUNKS, line)),
            dma((CHUNKS, line)),
            dma((CHUNKS, line)),
            dma((CHUNKS, group)),
            dma((CHUNKS, group)),
            dma((half // chans,)),
            dma((half // chans,)),
            dma,
        ],
        compiler_params=pltpu.CompilerParams(
            collective_id=0, has_side_effects=True, vmem_limit_bytes=60 << 20
        ),
        cost_estimate=pl.CostEstimate(
            flops=2 * stations * frames * nfft * 2 * total // sections,
            bytes_accessed=2 * stations * frames * nfft,
            transcendentals=0,
        ),
        name="beamformer",
    )(
        voltages.reshape(stations * frames, nfft),
        jnp.asarray(table),
        lut,
        index,
        measure,
        *(jnp.asarray(m) for m in matrices),
    )


def solution(mesh):
    in_specs = (P("dom", None, None), P(), P(), P(None, None, "dom"), P())
    out_specs = P(("section", "dom"), None, None)
    return jax.shard_map(body, mesh=mesh, in_specs=in_specs, out_specs=out_specs, check_vma=False)
```

```python
import functools
import math

import jax
import jax.numpy as jnp
import ml_dtypes
import numpy as np
from jax import lax
from jax.experimental import pallas as pl
from jax.experimental.pallas import tpu as pltpu
from jax.sharding import PartitionSpec as P

NTAB = 64
NDM = 32
LANES = 128
TILE = 16
PAIR = 2
CHUNKS = 8
PASSES = 2
ROWS = 256
PAD = 8
MESH = pl.DeviceIdType.MESH


def natural_channels(half, chunks):
    fine = half // (2 * chunks)
    chunk = np.arange(chunks)[:, None, None]
    side = np.arange(2)[None, :, None]
    return (side * (half // 2) + chunk * fine + np.arange(fine)[None, None, :]).reshape(chunks, 2 * fine)


def dft_rows(nfft, total, sections, chunks, passes):
    section = total // sections
    half = section // PAIR
    order = natural_channels(half, chunks).reshape(passes, -1)
    start = np.arange(sections)[:, None, None, None] * section
    chan = start + np.arange(PAIR)[None, None, :, None] * half + order[None, :, None, :]
    chan = chan.reshape(sections, passes, -1)
    sample = np.arange(nfft)
    window = (0.5 - 0.5 * np.cos(sample * (2.0 * math.pi / nfft))) / math.sqrt(nfft)
    angle = np.arange(nfft) * (2.0 * math.pi / nfft)
    cosine, sine = np.cos(angle), np.sin(angle)
    turn = chan[..., None] * sample % nfft
    rows = np.concatenate((cosine[turn] * window, -sine[turn] * window), axis=2)
    return rows.astype(np.float32).astype(ml_dtypes.bfloat16)


def split(values):
    values = values.astype(np.float32)
    high = values.astype(ml_dtypes.bfloat16)
    return high, (values - high.astype(np.float32)).astype(ml_dtypes.bfloat16)


def frame_matrices(frames):
    index = np.arange(frames)
    angle = (index[:, None] * index[None, :] % frames) * (2.0 * math.pi / frames)
    cosine, sine = np.cos(angle), np.sin(angle)
    real = np.concatenate((cosine, sine), axis=0)
    imag = np.concatenate((-sine, cosine), axis=0)
    forward = np.concatenate((real, imag, imag, real), axis=1)
    back_real = np.concatenate((cosine, -sine), axis=0)
    back_imag = np.concatenate((sine, cosine), axis=0)
    inverse = np.concatenate((back_real, back_imag), axis=1) / frames
    return split(forward) + split(inverse)


def pick_lanes(entries, where):
    dims = lax.GatherDimensionNumbers(
        offset_dims=(),
        collapsed_slice_dims=(1,),
        start_index_map=(1,),
        operand_batching_dims=(0,),
        start_indices_batching_dims=(0,),
    )
    return lax.gather(
        entries,
        where[..., None],
        dims,
        slice_sizes=(1, 1),
        mode=lax.GatherScatterMode.PROMISE_IN_BOUNDS,
    )


def dot(a, b):
    return jnp.dot(a, b, preferred_element_type=jnp.float32)


def cos_turns(turns):
    t = turns - jnp.round(turns)
    q = 0.25 - jnp.abs(t)
    x = q * q
    coeff = [(-1) ** k * (2.0 * math.pi) ** (2 * k + 1) / math.factorial(2 * k + 1) for k in range(7)]
    total = jnp.full_like(x, coeff[-1])
    for c in coeff[-2::-1]:
        total = total * x + c
    return total * q


def kernel(
    sections, doms, per, total,
    v_hbm, table_hbm, lut_ref, map_ref, beam_ref, trial_ref, fh_ref, fl_ref, gh_ref, gl_ref,
    out_ref,
    volts, table, lanes, ysend, x_buf, part, out_buf, in_right, in_left, sums, pw, rx, lut_rx, lut, where_ref, meas_ref,
    v_sem, t_sem, y_ss, y_rs, z_ss, zr_rs, zl_rs, p_ss, p_rs, l_ss, l_rs, l_sem, out_sem,
):
    s = lax.axis_index("section")
    d = lax.axis_index("dom")
    z = d // PAIR
    y = d % PAIR
    line = doms // PAIR
    group = sections * PAIR
    me = s * PAIR + y
    stations = ysend.shape[2]
    frames = LANES // 2
    chunks, _, count, beams, _ = part.shape
    half = chunks * count
    chans = lut_ref.shape[2]
    blocks = half // chans
    fine = count // 2
    tiles = volts.shape[0] // ROWS
    held = x_buf.shape[1]

    def load(tile):
        span = pl.ds(pl.multiple_of(tile * ROWS, ROWS), ROWS)
        return pltpu.make_async_copy(v_hbm.at[span], volts.at[span], v_sem.at[tile])

    def load_table(step):
        return pltpu.make_async_copy(table_hbm.at[s, step], table.at[step], t_sem.at[step])

    load_table(0).start()
    lax.fori_loop(0, tiles, lambda t, c: (load(t).start(), c)[1], 0)
    for step in range(1, PASSES):
        load_table(step).start()

    def node(g):
        return (g // PAIR, z * PAIR + g % PAIR)

    target_s = d // (blocks * PAIR)
    target_y = d // blocks % PAIR
    block_slot = d % blocks
    home_z = z % sections

    def lut_target(m):
        return (target_s, (m * sections + s) * PAIR + target_y)

    def lut_to_self(m):
        dev = lut_target(m)
        return (dev[0] == s) & (dev[1] == d)

    def lut_source(q):
        return (home_z, me * blocks + q)

    def lut_from_self(q):
        dev = lut_source(q)
        return (dev[0] == s) & (dev[1] == d)

    def lut_copy(m):
        return pltpu.make_async_remote_copy(
            src_ref=lut_ref,
            dst_ref=lut_rx.at[block_slot],
            send_sem=l_ss.at[m],
            recv_sem=l_rs.at[block_slot],
            device_id=lut_target(m),
            device_id_type=MESH,
        )

    def lut_wait(q):
        return pltpu.make_async_remote_copy(
            src_ref=lut_ref,
            dst_ref=lut_rx.at[q],
            send_sem=l_ss.at[0],
            recv_sem=l_rs.at[q],
            device_id=(s, d),
            device_id_type=MESH,
        )

    barrier = pltpu.get_barrier_semaphore()
    for k in range(1, group):
        pl.semaphore_signal(barrier, 1, device_id=node((me + k) % group), device_id_type=MESH)

    @pl.when(z > 0)
    def _():
        pl.semaphore_signal(barrier, 1, device_id=(s, d - PAIR), device_id_type=MESH)

    @pl.when(z < line - 1)
    def _():
        pl.semaphore_signal(barrier, 1, device_id=(s, d + PAIR), device_id_type=MESH)

    for q in range(blocks):

        @pl.when(jnp.logical_not(lut_from_self(q)))
        def _():
            pl.semaphore_signal(barrier, 1, device_id=lut_source(q), device_id_type=MESH)

    arrivals = group - 1 + (z > 0).astype(jnp.int32) + (z < line - 1).astype(jnp.int32)
    for m in range(blocks):
        arrivals = arrivals + jnp.logical_not(lut_to_self(m)).astype(jnp.int32)
    pl.semaphore_wait(barrier, arrivals)

    for m in range(blocks):

        @pl.when(jnp.logical_not(lut_to_self(m)))
        def _():
            lut_copy(m).start()

        @pl.when(lut_to_self(m))
        def _():
            own = pltpu.make_async_copy(lut_ref, lut_rx.at[block_slot], l_sem)
            own.start()
            own.wait()

    all_beams, everyone = beam_ref.shape
    stops = sections * line
    team = all_beams // stops
    row = map_ref[pl.ds(pl.multiple_of(z * held // LANES * LANES, LANES), LANES)].reshape(1, LANES)
    if held < LANES:
        row = pltpu.roll(jnp.broadcast_to(row, (8, LANES)), (LANES - z * held % LANES) % LANES, 1)[:1]
    here = (lax.broadcasted_iota(jnp.int32, (everyone, LANES), 0) == row).astype(jnp.float32)
    found = dot(beam_ref[...].astype(jnp.float32).astype(jnp.bfloat16), here.astype(jnp.bfloat16))
    ordered = [
        found[(at * line + to) * team : (at * line + to + 1) * team] for to in range(line) for at in range(sections)
    ]
    ordered = jnp.concatenate(ordered, axis=0).astype(jnp.int32)
    for part_at in range(2):
        where_ref[part_at] = (ordered + part_at * NTAB).astype(jnp.int16)
    for b in range(beams):
        trial = trial_ref[(b // team * line + z) * team + b % team]
        meas_ref[pl.ds(b, 1), :] = jnp.full((1, LANES), (trial + 1).astype(jnp.float32) * (1.0 / NDM), jnp.float32)

    first_half = lax.broadcasted_iota(jnp.int32, (1, LANES), 1) < frames
    half_rows = half // PASSES * PAIR
    pitch = lanes.shape[0] // half_rows
    chunk_pass = chunks // PASSES

    def y_copy(j):
        return pltpu.make_async_remote_copy(
            src_ref=ysend.at[j],
            dst_ref=x_buf.at[pl.ds(j * count, count), pl.ds(pl.multiple_of(y * stations, TILE), stations)],
            send_sem=y_ss.at[j],
            recv_sem=y_rs.at[j],
            device_id=(s, z * PAIR + 1 - y),
            device_id_type=MESH,
        )

    def channelise(step):
        load_table(step).wait()

        def tile_body(tile, carry):
            if step == 0:
                load(tile).wait()
            span = pl.ds(pl.multiple_of(tile * ROWS, ROWS), ROWS)
            o = lax.dot_general(
                table[step], volts[span], (((1,), (1,)), ((), ())), preferred_element_type=jnp.float32
            )
            for two in range(ROWS // LANES):
                a = o[:half_rows, two * LANES : (two + 1) * LANES]
                b = o[half_rows:, two * LANES : (two + 1) * LANES]
                even = jnp.where(first_half, a, pltpu.roll(b, frames, 1))
                odd = jnp.where(first_half, pltpu.roll(a, frames, 1), b)
                row = tile * (ROWS // frames) + two * 2
                lanes[pl.ds(row, half_rows, stride=pitch), :] = even
                lanes[pl.ds(row + 1, half_rows, stride=pitch), :] = odd
            return carry

        lax.fori_loop(0, tiles, tile_body, 0)

        def spectra(of, jj, cc):
            row = ((of * chunk_pass + jj) * count + cc) * pitch
            return lanes[pl.ds(row, stations), :].astype(jnp.bfloat16)

        def send_body(jj, carry):
            j = jj + step * chunk_pass
            for cc in range(count):
                ysend[j, cc] = spectra(1 - y, jj, cc)
            y_copy(j).start()
            return carry

        lax.fori_loop(0, chunk_pass, send_body, 0)

        def keep_body(jj, carry):
            j = jj + step * chunk_pass
            for cc in range(count):
                x_buf[j * count + cc, pl.ds(pl.multiple_of(y * stations, TILE), stations)] = spectra(y, jj, cc)
            return carry

        lax.fori_loop(0, chunk_pass, keep_body, 0)

    sign = jnp.where(first_half, -1.0, 1.0)

    def form(j):
        y_copy(j).wait_recv()

        def chan_body(fc, carry):
            for side in range(2):
                row = side * (half // 2) + j * fine + fc
                entry = jnp.broadcast_to(lut[pl.ds(row, 1), :].astype(jnp.bfloat16), (TILE, LANES))
                weights = jnp.concatenate(
                    [
                        pick_lanes(entry, where_ref[p, t * TILE : (t + 1) * TILE, :])
                        for p in range(2)
                        for t in range(where_ref.shape[1] // TILE)
                    ],
                    axis=0,
                )
                cc = side * fine + fc
                product = dot(weights[:, :held], x_buf[j * count + cc])
                beam = product[:all_beams] + sign * pltpu.roll(product[all_beams:], frames, 1)
                for to in range(line):
                    part[j, to, cc] = beam[to * beams : (to + 1) * beams]
            return carry

        lax.fori_loop(0, fine, chan_body, 0, unroll=4)

    def right_copy(j, to):
        return pltpu.make_async_remote_copy(
            src_ref=out_buf.at[j, to],
            dst_ref=in_right.at[j, to],
            send_sem=z_ss.at[j, to],
            recv_sem=zr_rs.at[j, to],
            device_id=(s, jnp.minimum(d + PAIR, doms - PAIR + y)),
            device_id_type=MESH,
        )

    def left_copy(j, to):
        return pltpu.make_async_remote_copy(
            src_ref=out_buf.at[j, to],
            dst_ref=in_left.at[j, to],
            send_sem=z_ss.at[j, to],
            recv_sem=zl_rs.at[j, to],
            device_id=(s, jnp.maximum(d - PAIR, y)),
            device_id_type=MESH,
        )

    def begin(j):
        for to in range(line - 1, 0, -1):

            @pl.when(z == 0)
            def _():
                out_buf[j, to] = part[j, to].astype(jnp.bfloat16)
                right_copy(j, to).start()

        for to in range(line - 1):

            @pl.when(z == line - 1)
            def _():
                out_buf[j, to] = part[j, to].astype(jnp.bfloat16)
                left_copy(j, to).start()

    def relay_right(j):
        for to in range(line - 1, 0, -1):

            @pl.when(z < to)
            def _():
                right_copy(j, to).wait_recv()
                out_buf[j, to] = (part[j, to] + in_right[j, to].astype(jnp.float32)).astype(jnp.bfloat16)
                right_copy(j, to).start()

    def relay_left(j):
        for to in range(line - 1):

            @pl.when(z > to)
            def _():
                left_copy(j, to).wait_recv()
                out_buf[j, to] = (part[j, to] + in_left[j, to].astype(jnp.float32)).astype(jnp.bfloat16)
                left_copy(j, to).start()

    def power_copy(j, k):
        g = (me + k) % group
        return pltpu.make_async_remote_copy(
            src_ref=pw.at[j, g],
            dst_ref=rx.at[me, j],
            send_sem=p_ss.at[j, k],
            recv_sem=p_rs.at[j, k],
            device_id=node(g),
            device_id_type=MESH,
        )

    lane = lax.broadcasted_iota(jnp.int32, (1, LANES), 1)
    bins = lane % frames
    kappa = jnp.where(bins < frames // 2, bins, bins - frames).astype(jnp.float32)
    turn_rate = kappa * kappa * (0.5 / frames)
    quarter = jnp.where(first_half, 0.0, 0.25)

    def finish(j):
        sums[...] = part[j, z].reshape(count * beams, LANES)

        @pl.when(z > 0)
        def _():
            right_copy(j, z).wait_recv()
            sums[...] += in_right[j, z].astype(jnp.float32).reshape(count * beams, LANES)

        @pl.when(z < line - 1)
        def _():
            left_copy(j, z).wait_recv()
            sums[...] += in_left[j, z].astype(jnp.float32).reshape(count * beams, LANES)

        within = lax.broadcasted_iota(jnp.int32, (count, LANES), 0)
        chan = me * half + within // fine * (half // 2) + j * fine + within % fine
        freq = 1.0 + chan.astype(jnp.float32) * (1.0 / total)
        rate = turn_rate / (freq * freq * freq)
        rows = [sums[pl.ds(b, count, stride=beams), :] for b in range(beams)]
        x = jnp.concatenate(rows, axis=0)
        high = x.astype(jnp.bfloat16)
        low = (x - high.astype(jnp.float32)).astype(jnp.bfloat16)
        spec = dot(high, fh_ref[...]) + dot(low, fh_ref[...]) + dot(high, fl_ref[...])
        turns = jnp.concatenate([meas_ref[b : b + 1, :] * rate - quarter for b in range(beams)], axis=0)
        chirp = cos_turns(turns)
        other = pltpu.roll(chirp, frames, 1)
        cosine = jnp.where(first_half, chirp, other)
        sine = jnp.where(first_half, -other, chirp)
        turned = spec[:, :LANES] * cosine + spec[:, LANES:] * sine
        high = turned.astype(jnp.bfloat16)
        low = (turned - high.astype(jnp.float32)).astype(jnp.bfloat16)
        series = dot(high, gh_ref[...]) + dot(low, gh_ref[...]) + dot(high, gl_ref[...])
        square = series * series
        power = square + pltpu.roll(square, frames, 1)
        power = power.reshape(beams, 2, fine, LANES)
        packed = jnp.where(first_half[None], power[:, 0], power[:, 1])
        pw[j] = packed.reshape(group, per * fine, LANES)
        for k in range(1, group):
            power_copy(j, k).start()
        rx[me, j] = pw[j, me]

    channelise(0)
    for q in range(blocks):

        @pl.when(jnp.logical_not(lut_from_self(q)))
        def _():
            lut_wait(q).wait_recv()

    for q in range(blocks):
        lut[pl.ds(q * chans, chans), :] = lut_rx[q].astype(jnp.float32).reshape(LANES, chans).T

    early = chunk_pass // 2
    late = line

    def step_body(i, carry):
        @pl.when(i < chunks)
        def _():
            form(i)
            begin(i)

        right_at = i - z
        left_at = i - (line - 1 - z)

        @pl.when((z > 0) & (right_at >= 0) & (right_at < chunks))
        def _():
            relay_right(right_at)

        @pl.when((z < line - 1) & (left_at >= 0) & (left_at < chunks))
        def _():
            relay_left(left_at)

        @pl.when(i >= late)
        def _():
            finish(i - late)

        return carry

    lax.fori_loop(0, early, step_body, 0)
    channelise(1)
    lax.fori_loop(early, chunks + late, step_body, 0)

    def drain(j, carry):
        y_copy(j).wait_send()
        for to in range(line):

            @pl.when(z < to)
            def _():
                right_copy(j, to).wait_send()

            @pl.when(z > to)
            def _():
                left_copy(j, to).wait_send()

        for k in range(1, group):
            power_copy(j, k).wait()
        return carry

    lax.fori_loop(0, chunks, drain, 0)
    for m in range(blocks):

        @pl.when(jnp.logical_not(lut_to_self(m)))
        def _():
            lut_copy(m).wait_send()

    result = pltpu.make_async_copy(rx, out_ref, out_sem)
    result.start()
    result.wait()


def arrange_kernel(x_ref, out_ref):
    group, chunks, fine, _ = x_ref.shape
    _, frames, _ = out_ref.shape
    for g in range(group):
        block = x_ref[g].reshape(chunks * fine, LANES).T
        half = 2 * chunks * fine
        out_ref[0, :, g * half : (g + 1) * half] = jnp.concatenate((block[:frames], block[frames:]), axis=1)


def arrange(x, frames, total):
    group, chunks, per, fine, _ = x.shape
    return pl.pallas_call(
        arrange_kernel,
        grid=(per,),
        in_specs=[pl.BlockSpec((group, chunks, None, fine, LANES), lambda i: (0, 0, i, 0, 0))],
        out_specs=pl.BlockSpec((1, frames, total), lambda i: (i, 0, 0)),
        out_shape=jax.ShapeDtypeStruct((per, frames, total), jnp.float32),
        name="arrange",
    )(x)


def body(voltages, station_map, beam_table, weight_table, dm_trial):
    sections = lax.axis_size("section")
    doms = lax.axis_size("dom")
    stations, frames, nfft = voltages.shape
    beams = beam_table.shape[0]
    chans = weight_table.shape[2]
    total = chans * doms
    line = doms // PAIR
    group = sections * PAIR
    per = beams // (sections * doms)
    half = total // group
    here = beams // line
    count = half // CHUNKS
    held = PAIR * stations

    table = dft_rows(nfft, total, sections, CHUNKS, PASSES)
    matrices = frame_matrices(frames)

    vmem = pl.BlockSpec(memory_space=pltpu.VMEM)
    hbm = pl.BlockSpec(memory_space=pl.ANY)
    dma = pltpu.SemaphoreType.DMA
    bf16, f32 = jnp.bfloat16, jnp.float32
    power = pl.pallas_call(
        functools.partial(kernel, sections, doms, per, total),
        in_specs=[hbm] * 3 + [vmem, vmem, pl.BlockSpec(memory_space=pltpu.SMEM)] + [vmem] * 4,
        out_specs=hbm,
        out_shape=jax.ShapeDtypeStruct((group, CHUNKS, per * count // 2, LANES), f32),
        scratch_shapes=[
            pltpu.VMEM((stations * frames, nfft), bf16),
            pltpu.VMEM(table.shape[1:], bf16),
            pltpu.VMEM((PAIR * half // PASSES * (stations + PAD), LANES), f32),
            pltpu.VMEM((CHUNKS, count, stations, LANES), bf16),
            pltpu.VMEM((half, held, LANES), bf16),
            pltpu.VMEM((CHUNKS, line, count, here, LANES), f32),
            pltpu.VMEM((CHUNKS, line, count, here, LANES), bf16),
            pltpu.VMEM((CHUNKS, line, count, here, LANES), bf16),
            pltpu.VMEM((CHUNKS, line, count, here, LANES), bf16),
            pltpu.VMEM((count * here, LANES), f32),
            pltpu.VMEM((CHUNKS, group, per * count // 2, LANES), f32),
            pltpu.VMEM((group, CHUNKS, per * count // 2, LANES), f32),
            pltpu.VMEM((half // chans,) + weight_table.shape, bf16),
            pltpu.VMEM((half, LANES), f32),
            pltpu.VMEM((2, beams, LANES), jnp.int16),
            pltpu.VMEM((here, LANES), f32),
            dma((stations * frames // ROWS,)),
            dma((PASSES,)),
            dma((CHUNKS,)),
            dma((CHUNKS,)),
            dma((CHUNKS, line)),
            dma((CHUNKS, line)),
            dma((CHUNKS, line)),
            dma((CHUNKS, group)),
            dma((CHUNKS, group)),
            dma((half // chans,)),
            dma((half // chans,)),
            dma,
            dma,
        ],
        compiler_params=pltpu.CompilerParams(
            collective_id=0, has_side_effects=True, vmem_limit_bytes=60 << 20
        ),
        cost_estimate=pl.CostEstimate(
            flops=2 * stations * frames * nfft * 2 * total // sections,
            bytes_accessed=2 * stations * frames * nfft,
            transcendentals=0,
        ),
        name="beamformer",
    )(
        voltages.reshape(stations * frames, nfft),
        jnp.asarray(table),
        weight_table,
        station_map,
        beam_table,
        dm_trial,
        *(jnp.asarray(m) for m in matrices),
    )
    return arrange(power.reshape(group, CHUNKS, per, count // 2, LANES), frames, total)


def solution(mesh):
    in_specs = (P("dom", None, None), P(), P(), P(None, None, "dom"), P())
    out_specs = P(("section", "dom"), None, None)
    return jax.shard_map(body, mesh=mesh, in_specs=in_specs, out_specs=out_specs, check_vma=False)
```

```python
import functools
import math

import jax
import jax.numpy as jnp
import ml_dtypes
import numpy as np
from jax import lax
from jax.experimental import pallas as pl
from jax.experimental.pallas import tpu as pltpu
from jax.sharding import PartitionSpec as P

NTAB = 64
NDM = 32
LANES = 128
TILE = 16
PAIR = 2
CHUNKS = 8
PASSES = 2
ROWS = 256
PAD = 8
GANG = 8
MESH = pl.DeviceIdType.MESH


def dft_rows(nfft, total, sections, passes):
    section = total // sections
    half = section // PAIR
    order = np.arange(half).reshape(passes, -1)
    start = np.arange(sections)[:, None, None, None] * section
    chan = start + np.arange(PAIR)[None, None, :, None] * half + order[None, :, None, :]
    chan = chan.reshape(sections, passes, -1)
    sample = np.arange(nfft)
    window = (0.5 - 0.5 * np.cos(sample * (2.0 * math.pi / nfft))) / math.sqrt(nfft)
    angle = np.arange(nfft) * (2.0 * math.pi / nfft)
    cosine, sine = np.cos(angle), np.sin(angle)
    turn = chan[..., None] * sample % nfft
    rows = np.concatenate((cosine[turn] * window, -sine[turn] * window), axis=2)
    return rows.astype(np.float32).astype(ml_dtypes.bfloat16)


def split(values):
    values = values.astype(np.float32)
    high = values.astype(ml_dtypes.bfloat16)
    return high, (values - high.astype(np.float32)).astype(ml_dtypes.bfloat16)


def frame_matrices(frames):
    index = np.arange(frames)
    angle = (index[:, None] * index[None, :] % frames) * (2.0 * math.pi / frames)
    cosine, sine = np.cos(angle), np.sin(angle)
    real = np.concatenate((cosine, sine), axis=0)
    imag = np.concatenate((-sine, cosine), axis=0)
    forward = np.concatenate((real, imag, imag, real), axis=1)
    back_real = np.concatenate((cosine, -sine), axis=0)
    back_imag = np.concatenate((sine, cosine), axis=0)
    inverse = np.concatenate((back_real, back_imag), axis=1) / frames
    return split(forward) + split(inverse)


def pick_lanes(entries, where):
    dims = lax.GatherDimensionNumbers(
        offset_dims=(),
        collapsed_slice_dims=(1,),
        start_index_map=(1,),
        operand_batching_dims=(0,),
        start_indices_batching_dims=(0,),
    )
    return lax.gather(
        entries,
        where[..., None],
        dims,
        slice_sizes=(1, 1),
        mode=lax.GatherScatterMode.PROMISE_IN_BOUNDS,
    )


def dot(a, b):
    return jnp.dot(a, b, preferred_element_type=jnp.float32)


def cos_turns(turns):
    t = turns - jnp.round(turns)
    q = 0.25 - jnp.abs(t)
    x = q * q
    coeff = [(-1) ** k * (2.0 * math.pi) ** (2 * k + 1) / math.factorial(2 * k + 1) for k in range(7)]
    total = jnp.full_like(x, coeff[-1])
    for c in coeff[-2::-1]:
        total = total * x + c
    return total * q


def kernel(
    sections, doms, per, total,
    v_hbm, table_hbm, lut_ref, map_ref, beam_ref, trial_ref, fh_ref, fl_ref, gh_ref, gl_ref,
    out_ref,
    volts, table, lanes, ysend, x_buf, part, out_buf, in_right, in_left, sums, pw, rx, lut_rx, lut, where_ref, meas_ref,
    v_sem, t_sem, y_ss, y_rs, z_ss, zr_rs, zl_rs, p_ss, p_rs, l_ss, l_rs, l_sem, out_sem,
):
    s = lax.axis_index("section")
    d = lax.axis_index("dom")
    z = d // PAIR
    y = d % PAIR
    line = doms // PAIR
    group = sections * PAIR
    me = s * PAIR + y
    stations = ysend.shape[2]
    frames = LANES // 2
    chunks, _, count, beams, _ = part.shape
    half = chunks * count
    chans = lut_ref.shape[2]
    blocks = half // chans
    pack = 2 - per % 2
    tiles = volts.shape[0] // ROWS
    held = x_buf.shape[1]

    def load(tile):
        span = pl.ds(pl.multiple_of(tile * ROWS, ROWS), ROWS)
        return pltpu.make_async_copy(v_hbm.at[span], volts.at[span], v_sem.at[tile])

    def load_table(step):
        return pltpu.make_async_copy(table_hbm.at[s, step], table.at[step], t_sem.at[step])

    load_table(0).start()
    lax.fori_loop(0, tiles, lambda t, c: (load(t).start(), c)[1], 0)
    for step in range(1, PASSES):
        load_table(step).start()

    def node(g):
        return (g // PAIR, z * PAIR + g % PAIR)

    target_s = d // (blocks * PAIR)
    target_y = d // blocks % PAIR
    block_slot = d % blocks
    home_z = z % sections

    def lut_target(m):
        return (target_s, (m * sections + s) * PAIR + target_y)

    def lut_to_self(m):
        dev = lut_target(m)
        return (dev[0] == s) & (dev[1] == d)

    def lut_source(q):
        return (home_z, me * blocks + q)

    def lut_from_self(q):
        dev = lut_source(q)
        return (dev[0] == s) & (dev[1] == d)

    def lut_copy(m):
        return pltpu.make_async_remote_copy(
            src_ref=lut_ref,
            dst_ref=lut_rx.at[block_slot],
            send_sem=l_ss.at[m],
            recv_sem=l_rs.at[block_slot],
            device_id=lut_target(m),
            device_id_type=MESH,
        )

    def lut_wait(q):
        return pltpu.make_async_remote_copy(
            src_ref=lut_ref,
            dst_ref=lut_rx.at[q],
            send_sem=l_ss.at[0],
            recv_sem=l_rs.at[q],
            device_id=(s, d),
            device_id_type=MESH,
        )

    barrier = pltpu.get_barrier_semaphore()
    for k in range(1, group):
        pl.semaphore_signal(barrier, 1, device_id=node((me + k) % group), device_id_type=MESH)

    @pl.when(z > 0)
    def _():
        pl.semaphore_signal(barrier, 1, device_id=(s, d - PAIR), device_id_type=MESH)

    @pl.when(z < line - 1)
    def _():
        pl.semaphore_signal(barrier, 1, device_id=(s, d + PAIR), device_id_type=MESH)

    for q in range(blocks):

        @pl.when(jnp.logical_not(lut_from_self(q)))
        def _():
            pl.semaphore_signal(barrier, 1, device_id=lut_source(q), device_id_type=MESH)

    arrivals = group - 1 + (z > 0).astype(jnp.int32) + (z < line - 1).astype(jnp.int32)
    for m in range(blocks):
        arrivals = arrivals + jnp.logical_not(lut_to_self(m)).astype(jnp.int32)

    all_beams, everyone = beam_ref.shape
    stops = sections * line
    team = all_beams // stops
    row = map_ref[pl.ds(pl.multiple_of(z * held // LANES * LANES, LANES), LANES)].reshape(1, LANES)
    if held < LANES:
        row = pltpu.roll(jnp.broadcast_to(row, (8, LANES)), (LANES - z * held % LANES) % LANES, 1)[:1]
    here = (lax.broadcasted_iota(jnp.int32, (everyone, LANES), 0) == row).astype(jnp.float32)
    found = dot(beam_ref[...].astype(jnp.float32).astype(jnp.bfloat16), here.astype(jnp.bfloat16))
    ordered = [
        found[(at * line + to) * team : (at * line + to + 1) * team] for to in range(line) for at in range(sections)
    ]
    ordered = jnp.concatenate(ordered, axis=0).astype(jnp.int32)
    for part_at in range(2):
        where_ref[part_at] = (ordered + part_at * NTAB).astype(jnp.int16)
    for b in range(beams):
        trial = trial_ref[(b // team * line + z) * team + b % team]
        meas_ref[pl.ds(b, 1), :] = jnp.full((1, LANES), (trial + 1).astype(jnp.float32) * (1.0 / NDM), jnp.float32)

    def enter():
        pl.semaphore_wait(barrier, arrivals)
        for m in range(blocks):

            @pl.when(jnp.logical_not(lut_to_self(m)))
            def _():
                lut_copy(m).start()

            @pl.when(lut_to_self(m))
            def _():
                own = pltpu.make_async_copy(lut_ref, lut_rx.at[block_slot], l_sem)
                own.start()
                own.wait()

    first_half = lax.broadcasted_iota(jnp.int32, (1, LANES), 1) < frames
    half_rows = half // PASSES * PAIR
    pitch = lanes.shape[0] // half_rows
    chunk_pass = chunks // PASSES

    def y_copy(j):
        return pltpu.make_async_remote_copy(
            src_ref=ysend.at[j],
            dst_ref=x_buf.at[pl.ds(j * count, count), pl.ds(pl.multiple_of(y * stations, TILE), stations)],
            send_sem=y_ss.at[j],
            recv_sem=y_rs.at[j],
            device_id=(s, z * PAIR + 1 - y),
            device_id_type=MESH,
        )

    def channelise(step):
        load_table(step).wait()

        def tile_body(tile, carry):
            if step == 0:
                load(tile).wait()
            span = pl.ds(pl.multiple_of(tile * ROWS, ROWS), ROWS)
            o = lax.dot_general(
                table[step], volts[span], (((1,), (1,)), ((), ())), preferred_element_type=jnp.float32
            )
            for two in range(ROWS // LANES):
                a = o[:half_rows, two * LANES : (two + 1) * LANES]
                b = o[half_rows:, two * LANES : (two + 1) * LANES]
                even = jnp.where(first_half, a, pltpu.roll(b, frames, 1))
                odd = jnp.where(first_half, pltpu.roll(a, frames, 1), b)
                row = tile * (ROWS // frames) + two * 2
                lanes[pl.ds(row, half_rows, stride=pitch), :] = even
                lanes[pl.ds(row + 1, half_rows, stride=pitch), :] = odd
            return carry

        lax.fori_loop(0, tiles, tile_body, 0)
        if step == 0:
            enter()

        def spectra(of, jj, cc):
            row = ((of * chunk_pass + jj) * count + cc) * pitch
            return lanes[pl.ds(row, stations), :].astype(jnp.bfloat16)

        def send_body(jj, carry):
            j = jj + step * chunk_pass
            for cc in range(count):
                ysend[j, cc] = spectra(1 - y, jj, cc)
            y_copy(j).start()
            return carry

        lax.fori_loop(0, chunk_pass, send_body, 0)

        def keep_body(jj, carry):
            j = jj + step * chunk_pass
            for cc in range(count):
                x_buf[j * count + cc, pl.ds(pl.multiple_of(y * stations, TILE), stations)] = spectra(y, jj, cc)
            return carry

        lax.fori_loop(0, chunk_pass, keep_body, 0)

    sign = jnp.where(first_half, -1.0, 1.0)

    def form(j):
        y_copy(j).wait_recv()

        def chan_body(at, carry):
            for step in range(GANG):
                cc = at * GANG + step
                row = j * count + cc
                entry = jnp.broadcast_to(lut[pl.ds(row, 1), :].astype(jnp.bfloat16), (TILE, LANES))
                weights = jnp.concatenate(
                    [
                        pick_lanes(entry, where_ref[p, t * TILE : (t + 1) * TILE, :])
                        for p in range(2)
                        for t in range(where_ref.shape[1] // TILE)
                    ],
                    axis=0,
                )
                product = dot(weights[:, :held], x_buf[row])
                beam = product[:all_beams] + sign * pltpu.roll(product[all_beams:], frames, 1)
                for to in range(line):
                    part[j, to, cc] = beam[to * beams : (to + 1) * beams]
            return carry

        lax.fori_loop(0, count // GANG, chan_body, 0)

    def right_copy(j, to):
        return pltpu.make_async_remote_copy(
            src_ref=out_buf.at[j, to],
            dst_ref=in_right.at[j, to],
            send_sem=z_ss.at[j, to],
            recv_sem=zr_rs.at[j, to],
            device_id=(s, jnp.minimum(d + PAIR, doms - PAIR + y)),
            device_id_type=MESH,
        )

    def left_copy(j, to):
        return pltpu.make_async_remote_copy(
            src_ref=out_buf.at[j, to],
            dst_ref=in_left.at[j, to],
            send_sem=z_ss.at[j, to],
            recv_sem=zl_rs.at[j, to],
            device_id=(s, jnp.maximum(d - PAIR, y)),
            device_id_type=MESH,
        )

    def begin(j):
        for to in range(line - 1, 0, -1):

            @pl.when(z == 0)
            def _():
                out_buf[j, to] = part[j, to].astype(jnp.bfloat16)
                right_copy(j, to).start()

        for to in range(line - 1):

            @pl.when(z == line - 1)
            def _():
                out_buf[j, to] = part[j, to].astype(jnp.bfloat16)
                left_copy(j, to).start()

    def relay_right(j):
        for to in range(line - 1, 0, -1):

            @pl.when(z < to)
            def _():
                right_copy(j, to).wait_recv()
                out_buf[j, to] = (part[j, to] + in_right[j, to].astype(jnp.float32)).astype(jnp.bfloat16)
                right_copy(j, to).start()

    def relay_left(j):
        for to in range(line - 1):

            @pl.when(z > to)
            def _():
                left_copy(j, to).wait_recv()
                out_buf[j, to] = (part[j, to] + in_left[j, to].astype(jnp.float32)).astype(jnp.bfloat16)
                left_copy(j, to).start()

    def power_copy(j, k):
        g = (me + k) % group
        return pltpu.make_async_remote_copy(
            src_ref=pw.at[j, g],
            dst_ref=rx.at[me, j],
            send_sem=p_ss.at[j],
            recv_sem=p_rs.at[j],
            device_id=node(g),
            device_id_type=MESH,
        )

    def power_all(j):
        return pltpu.make_async_remote_copy(
            src_ref=pw.at[j, pl.ds(0, group - 1)],
            dst_ref=rx.at[pl.ds(0, group - 1), j],
            send_sem=p_ss.at[j],
            recv_sem=p_rs.at[j],
            device_id=node((me + 1) % group),
            device_id_type=MESH,
        )

    lane = lax.broadcasted_iota(jnp.int32, (1, LANES), 1)
    bins = lane % frames
    kappa = jnp.where(bins < frames // 2, bins, bins - frames).astype(jnp.float32)
    turn_rate = kappa * kappa * (0.5 / frames)
    quarter = jnp.where(first_half, 0.0, 0.25)

    def finish(j):
        sums[...] = part[j, z].reshape(count * beams, LANES)

        @pl.when(z > 0)
        def _():
            right_copy(j, z).wait_recv()
            sums[...] += in_right[j, z].astype(jnp.float32).reshape(count * beams, LANES)

        @pl.when(z < line - 1)
        def _():
            left_copy(j, z).wait_recv()
            sums[...] += in_left[j, z].astype(jnp.float32).reshape(count * beams, LANES)

        within = lax.broadcasted_iota(jnp.int32, (count, LANES), 0)
        chan = me * half + j * count + within
        freq = 1.0 + chan.astype(jnp.float32) * (1.0 / total)
        rate = turn_rate / (freq * freq * freq)
        rows = [sums[pl.ds(b, count, stride=beams), :] for b in range(beams)]
        x = jnp.concatenate(rows, axis=0)
        high = x.astype(jnp.bfloat16)
        low = (x - high.astype(jnp.float32)).astype(jnp.bfloat16)
        spec = dot(high, fh_ref[...]) + dot(low, fh_ref[...]) + dot(high, fl_ref[...])
        turns = jnp.concatenate([meas_ref[b : b + 1, :] * rate - quarter for b in range(beams)], axis=0)
        chirp = cos_turns(turns)
        other = pltpu.roll(chirp, frames, 1)
        cosine = jnp.where(first_half, chirp, other)
        sine = jnp.where(first_half, -other, chirp)
        turned = spec[:, :LANES] * cosine + spec[:, LANES:] * sine
        high = turned.astype(jnp.bfloat16)
        low = (turned - high.astype(jnp.float32)).astype(jnp.bfloat16)
        series = dot(high, gh_ref[...]) + dot(low, gh_ref[...]) + dot(high, gl_ref[...])
        square = series * series
        power = square + pltpu.roll(square, frames, 1)
        if pack == 2:
            power = power.reshape(beams // 2, 2, count, LANES)
            power = jnp.where(first_half[None], power[:, 0], power[:, 1])
        pw[j] = power.reshape(group, per // pack * count, LANES)
        for k in range(1, group):
            power_copy(j, k).start()
        rx[me, j] = pw[j, me]

    channelise(0)
    for q in range(blocks):

        @pl.when(jnp.logical_not(lut_from_self(q)))
        def _():
            lut_wait(q).wait_recv()

    for q in range(blocks):
        lut[pl.ds(q * chans, chans), :] = lut_rx[q].astype(jnp.float32).reshape(LANES, chans).T

    def drain(j):
        y_copy(j).wait_send()
        for to in range(line):

            @pl.when(z < to)
            def _():
                right_copy(j, to).wait_send()

            @pl.when(z > to)
            def _():
                left_copy(j, to).wait_send()

        power_all(j).wait()
    early = chunk_pass // 2
    late = line

    def step_body(i, carry):
        @pl.when(i < chunks)
        def _():
            form(i)
            begin(i)

        right_at = i - z
        left_at = i - (line - 1 - z)

        @pl.when((z > 0) & (right_at >= 0) & (right_at < chunks))
        def _():
            relay_right(right_at)

        @pl.when((z < line - 1) & (left_at >= 0) & (left_at < chunks))
        def _():
            relay_left(left_at)

        @pl.when(i >= late)
        def _():
            finish(i - late)

        @pl.when(i >= late + 2)
        def _():
            drain(i - late - 2)

        return carry

    lax.fori_loop(0, early, step_body, 0)
    channelise(1)
    lax.fori_loop(early, chunks + late, step_body, 0)
    for j in range(chunks - 2, chunks):
        drain(j)

    for m in range(blocks):

        @pl.when(jnp.logical_not(lut_to_self(m)))
        def _():
            lut_copy(m).wait_send()

    result = pltpu.make_async_copy(rx, out_ref, out_sem)
    result.start()
    result.wait()


def arrange_kernel(x_ref, out_ref):
    group, chunks, rows, _ = x_ref.shape
    per, frames, _ = out_ref.shape
    pack = 2 - per % 2
    count = rows * pack // per
    half = chunks * count
    for g in range(group):
        for b in range(per // pack):
            block = x_ref[g, :, b * count : (b + 1) * count, :].reshape(half, LANES).T
            for part in range(pack):
                at = pl.ds(g * half, half)
                out_ref[b * pack + part, :, at] = block[part * frames : (part + 1) * frames]


def arrange(x, per, frames, total):
    vmem = pl.BlockSpec(memory_space=pltpu.VMEM)
    return pl.pallas_call(
        arrange_kernel,
        in_specs=[vmem],
        out_specs=vmem,
        out_shape=jax.ShapeDtypeStruct((per, frames, total), jnp.float32),
        name="arrange",
    )(x)


def body(voltages, station_map, beam_table, weight_table, dm_trial):
    sections = lax.axis_size("section")
    doms = lax.axis_size("dom")
    stations, frames, nfft = voltages.shape
    beams = beam_table.shape[0]
    chans = weight_table.shape[2]
    total = chans * doms
    line = doms // PAIR
    group = sections * PAIR
    per = beams // (sections * doms)
    half = total // group
    here = beams // line
    count = half // CHUNKS
    held = PAIR * stations

    table = dft_rows(nfft, total, sections, PASSES)
    matrices = frame_matrices(frames)

    vmem = pl.BlockSpec(memory_space=pltpu.VMEM)
    hbm = pl.BlockSpec(memory_space=pl.ANY)
    dma = pltpu.SemaphoreType.DMA
    bf16, f32 = jnp.bfloat16, jnp.float32
    power = pl.pallas_call(
        functools.partial(kernel, sections, doms, per, total),
        in_specs=[hbm] * 3 + [vmem, vmem, pl.BlockSpec(memory_space=pltpu.SMEM)] + [vmem] * 4,
        out_specs=hbm,
        out_shape=jax.ShapeDtypeStruct((group, CHUNKS, per * count // (2 - per % 2), LANES), f32),
        scratch_shapes=[
            pltpu.VMEM((stations * frames, nfft), bf16),
            pltpu.VMEM(table.shape[1:], bf16),
            pltpu.VMEM((PAIR * half // PASSES * (stations + PAD), LANES), f32),
            pltpu.VMEM((CHUNKS, count, stations, LANES), bf16),
            pltpu.VMEM((half, held, LANES), bf16),
            pltpu.VMEM((CHUNKS, line, count, here, LANES), f32),
            pltpu.VMEM((CHUNKS, line, count, here, LANES), bf16),
            pltpu.VMEM((CHUNKS, line, count, here, LANES), bf16),
            pltpu.VMEM((CHUNKS, line, count, here, LANES), bf16),
            pltpu.VMEM((count * here, LANES), f32),
            pltpu.VMEM((CHUNKS, group, per * count // (2 - per % 2), LANES), f32),
            pltpu.VMEM((group, CHUNKS, per * count // (2 - per % 2), LANES), f32),
            pltpu.VMEM((half // chans,) + weight_table.shape, bf16),
            pltpu.VMEM((half, LANES), f32),
            pltpu.VMEM((2, beams, LANES), jnp.int16),
            pltpu.VMEM((here, LANES), f32),
            dma((stations * frames // ROWS,)),
            dma((PASSES,)),
            dma((CHUNKS,)),
            dma((CHUNKS,)),
            dma((CHUNKS, line)),
            dma((CHUNKS, line)),
            dma((CHUNKS, line)),
            dma((CHUNKS,)),
            dma((CHUNKS,)),
            dma((half // chans,)),
            dma((half // chans,)),
            dma,
            dma,
        ],
        compiler_params=pltpu.CompilerParams(
            collective_id=0, has_side_effects=True, vmem_limit_bytes=60 << 20
        ),
        cost_estimate=pl.CostEstimate(
            flops=2 * stations * frames * nfft * 2 * total // sections,
            bytes_accessed=2 * stations * frames * nfft,
            transcendentals=0,
        ),
        name="beamformer",
    )(
        voltages.reshape(stations * frames, nfft),
        jnp.asarray(table),
        weight_table,
        station_map,
        beam_table,
        dm_trial,
        *(jnp.asarray(m) for m in matrices),
    )
    return arrange(power, per, frames, total)


def solution(mesh):
    in_specs = (P("dom", None, None), P(), P(), P(None, None, "dom"), P())
    out_specs = P(("section", "dom"), None, None)
    return jax.shard_map(body, mesh=mesh, in_specs=in_specs, out_specs=out_specs, check_vma=False)
```

```python
import functools
import math

import jax
import jax.numpy as jnp
import ml_dtypes
import numpy as np
from jax import lax
from jax.experimental import pallas as pl
from jax.experimental.pallas import tpu as pltpu
from jax.sharding import PartitionSpec as P

NTAB = 64
NDM = 32
LANES = 128
TILE = 16
PAIR = 2
CHUNKS = 8
PASSES = 2
ROWS = 1024
PAD = 8
GANG = 8
MESH = pl.DeviceIdType.MESH


def dft_rows(nfft, total, sections, passes):
    section = total // sections
    half = section // PAIR
    order = np.arange(half).reshape(passes, -1)
    start = np.arange(sections)[:, None, None, None] * section
    chan = start + np.arange(PAIR)[None, None, :, None] * half + order[None, :, None, :]
    chan = chan.reshape(sections, passes, -1)
    sample = np.arange(nfft)
    window = (0.5 - 0.5 * np.cos(sample * (2.0 * math.pi / nfft))) / math.sqrt(nfft)
    angle = np.arange(nfft) * (2.0 * math.pi / nfft)
    cosine, sine = np.cos(angle), np.sin(angle)
    turn = chan[..., None] * sample % nfft
    rows = np.concatenate((cosine[turn] * window, -sine[turn] * window), axis=2)
    return rows.astype(np.float32).astype(ml_dtypes.bfloat16)


def split(values):
    values = values.astype(np.float32)
    high = values.astype(ml_dtypes.bfloat16)
    return high, (values - high.astype(np.float32)).astype(ml_dtypes.bfloat16)


def frame_matrices(frames):
    index = np.arange(frames)
    angle = (index[:, None] * index[None, :] % frames) * (2.0 * math.pi / frames)
    cosine, sine = np.cos(angle), np.sin(angle)
    real = np.concatenate((cosine, sine), axis=0)
    imag = np.concatenate((-sine, cosine), axis=0)
    forward = np.concatenate((real, imag, imag, real), axis=1)
    back_real = np.concatenate((cosine, -sine), axis=0)
    back_imag = np.concatenate((sine, cosine), axis=0)
    inverse = np.concatenate((back_real, back_imag), axis=1) / frames
    return split(forward) + split(inverse)


def pick_lanes(entries, where):
    dims = lax.GatherDimensionNumbers(
        offset_dims=(),
        collapsed_slice_dims=(1,),
        start_index_map=(1,),
        operand_batching_dims=(0,),
        start_indices_batching_dims=(0,),
    )
    return lax.gather(
        entries,
        where[..., None],
        dims,
        slice_sizes=(1, 1),
        mode=lax.GatherScatterMode.PROMISE_IN_BOUNDS,
    )


def dot(a, b):
    return jnp.dot(a, b, preferred_element_type=jnp.float32)


def cos_turns(turns):
    t = turns - jnp.round(turns)
    q = 0.25 - jnp.abs(t)
    x = q * q
    coeff = [(-1) ** k * (2.0 * math.pi) ** (2 * k + 1) / math.factorial(2 * k + 1) for k in range(7)]
    total = jnp.full_like(x, coeff[-1])
    for c in coeff[-2::-1]:
        total = total * x + c
    return total * q


def kernel(
    sections, doms, per, total,
    v_hbm, table_hbm, lut_ref, map_ref, beam_ref, trial_ref, fh_ref, fl_ref, gh_ref, gl_ref,
    out_ref,
    volts, table, lanes, ysend, x_buf, part, out_buf, in_right, in_left, sums, pw, rx, lut_rx, lut, where_ref, meas_ref,
    v_sem, t_sem, y_ss, y_rs, z_ss, zr_rs, zl_rs, p_ss, p_rs, l_ss, l_rs, l_sem, out_sem,
):
    s = lax.axis_index("section")
    d = lax.axis_index("dom")
    z = d // PAIR
    y = d % PAIR
    line = doms // PAIR
    group = sections * PAIR
    me = s * PAIR + y
    stations = ysend.shape[2]
    frames = LANES // 2
    chunks, _, count, beams, _ = part.shape
    half = chunks * count
    chans = lut_ref.shape[2]
    blocks = half // chans
    pack = 2 - per % 2
    tiles = volts.shape[0] // ROWS
    held = x_buf.shape[1]

    def load(tile):
        span = pl.ds(pl.multiple_of(tile * ROWS, ROWS), ROWS)
        return pltpu.make_async_copy(v_hbm.at[span], volts.at[span], v_sem.at[tile])

    def load_table(step):
        return pltpu.make_async_copy(table_hbm.at[s, step], table.at[step], t_sem.at[step])

    load_table(0).start()
    lax.fori_loop(0, tiles, lambda t, c: (load(t).start(), c)[1], 0)
    for step in range(1, PASSES):
        load_table(step).start()

    def node(g):
        return (g // PAIR, z * PAIR + g % PAIR)

    target_s = d // (blocks * PAIR)
    target_y = d // blocks % PAIR
    block_slot = d % blocks
    home_z = z % sections

    def lut_target(m):
        return (target_s, (m * sections + s) * PAIR + target_y)

    def lut_to_self(m):
        dev = lut_target(m)
        return (dev[0] == s) & (dev[1] == d)

    def lut_source(q):
        return (home_z, me * blocks + q)

    def lut_from_self(q):
        dev = lut_source(q)
        return (dev[0] == s) & (dev[1] == d)

    def lut_copy(m):
        return pltpu.make_async_remote_copy(
            src_ref=lut_ref,
            dst_ref=lut_rx.at[block_slot],
            send_sem=l_ss.at[m],
            recv_sem=l_rs.at[block_slot],
            device_id=lut_target(m),
            device_id_type=MESH,
        )

    def lut_wait(q):
        return pltpu.make_async_remote_copy(
            src_ref=lut_ref,
            dst_ref=lut_rx.at[q],
            send_sem=l_ss.at[0],
            recv_sem=l_rs.at[q],
            device_id=(s, d),
            device_id_type=MESH,
        )

    barrier = pltpu.get_barrier_semaphore()
    for k in range(1, group):
        pl.semaphore_signal(barrier, 1, device_id=node((me + k) % group), device_id_type=MESH)

    @pl.when(z > 0)
    def _():
        pl.semaphore_signal(barrier, 1, device_id=(s, d - PAIR), device_id_type=MESH)

    @pl.when(z < line - 1)
    def _():
        pl.semaphore_signal(barrier, 1, device_id=(s, d + PAIR), device_id_type=MESH)

    for q in range(blocks):

        @pl.when(jnp.logical_not(lut_from_self(q)))
        def _():
            pl.semaphore_signal(barrier, 1, device_id=lut_source(q), device_id_type=MESH)

    arrivals = group - 1 + (z > 0).astype(jnp.int32) + (z < line - 1).astype(jnp.int32)
    for m in range(blocks):
        arrivals = arrivals + jnp.logical_not(lut_to_self(m)).astype(jnp.int32)

    all_beams, everyone = beam_ref.shape
    stops = sections * line
    team = all_beams // stops
    row = map_ref[pl.ds(pl.multiple_of(z * held // LANES * LANES, LANES), LANES)].reshape(1, LANES)
    if held < LANES:
        row = pltpu.roll(jnp.broadcast_to(row, (8, LANES)), (LANES - z * held % LANES) % LANES, 1)[:1]
    here = (lax.broadcasted_iota(jnp.int32, (everyone, LANES), 0) == row).astype(jnp.float32)
    found = dot(beam_ref[...].astype(jnp.float32).astype(jnp.bfloat16), here.astype(jnp.bfloat16))
    ordered = [
        found[(at * line + to) * team : (at * line + to + 1) * team] for to in range(line) for at in range(sections)
    ]
    ordered = jnp.concatenate(ordered, axis=0).astype(jnp.int32)
    for part_at in range(2):
        where_ref[part_at] = (ordered + part_at * NTAB).astype(jnp.int16)
    for b in range(beams):
        trial = trial_ref[(b // team * line + z) * team + b % team]
        meas_ref[pl.ds(b, 1), :] = jnp.full((1, LANES), (trial + 1).astype(jnp.float32) * (1.0 / NDM), jnp.float32)

    def enter():
        pl.semaphore_wait(barrier, arrivals)
        for m in range(blocks):

            @pl.when(jnp.logical_not(lut_to_self(m)))
            def _():
                lut_copy(m).start()

            @pl.when(lut_to_self(m))
            def _():
                own = pltpu.make_async_copy(lut_ref, lut_rx.at[block_slot], l_sem)
                own.start()
                own.wait()

    first_half = lax.broadcasted_iota(jnp.int32, (1, LANES), 1) < frames
    half_rows = half // PASSES * PAIR
    pitch = lanes.shape[0] // half_rows
    chunk_pass = chunks // PASSES

    gangs = count // GANG

    def y_copy(j, g):
        return pltpu.make_async_remote_copy(
            src_ref=ysend.at[j, pl.ds(g * GANG, GANG)],
            dst_ref=x_buf.at[pl.ds(j * count + g * GANG, GANG), pl.ds(pl.multiple_of(y * stations, TILE), stations)],
            send_sem=y_ss.at[j, g],
            recv_sem=y_rs.at[j, g],
            device_id=(s, z * PAIR + 1 - y),
            device_id_type=MESH,
        )

    def channelise(step):
        load_table(step).wait()

        def tile_body(tile, carry):
            if step == 0:
                load(tile).wait()
            span = pl.ds(pl.multiple_of(tile * ROWS, ROWS), ROWS)
            o = lax.dot_general(
                table[step], volts[span], (((1,), (1,)), ((), ())), preferred_element_type=jnp.float32
            )
            for two in range(ROWS // LANES):
                a = o[:half_rows, two * LANES : (two + 1) * LANES]
                b = o[half_rows:, two * LANES : (two + 1) * LANES]
                even = jnp.where(first_half, a, pltpu.roll(b, frames, 1))
                odd = jnp.where(first_half, pltpu.roll(a, frames, 1), b)
                row = tile * (ROWS // frames) + two * (LANES // frames)
                lanes[pl.ds(row, half_rows, stride=pitch), :] = even
                lanes[pl.ds(row + 1, half_rows, stride=pitch), :] = odd
            return carry

        lax.fori_loop(0, tiles, tile_body, 0)
        if step == 0:
            enter()

        def spectra(of, jj, cc):
            row = ((of * chunk_pass + jj) * count + cc) * pitch
            return lanes[pl.ds(row, stations), :].astype(jnp.bfloat16)

        def send_body(jj, carry):
            j = jj + step * chunk_pass
            for cc in range(count):
                ysend[j, cc] = spectra(1 - y, jj, cc)
                if (cc + 1) % GANG == 0:
                    y_copy(j, cc // GANG).start()
            return carry

        lax.fori_loop(0, chunk_pass, send_body, 0)

        def keep_body(jj, carry):
            j = jj + step * chunk_pass
            for cc in range(count):
                x_buf[j * count + cc, pl.ds(pl.multiple_of(y * stations, TILE), stations)] = spectra(y, jj, cc)
            return carry

        lax.fori_loop(0, chunk_pass, keep_body, 0)

    sign = jnp.where(first_half, -1.0, 1.0)

    def form(j):
        def chan_body(at, carry):
            y_copy(j, at).wait_recv()
            for step in range(GANG):
                cc = at * GANG + step
                row = j * count + cc
                entry = jnp.broadcast_to(lut[pl.ds(row, 1), :].astype(jnp.bfloat16), (TILE, LANES))
                weights = jnp.concatenate(
                    [
                        pick_lanes(entry, where_ref[p, t * TILE : (t + 1) * TILE, :])
                        for p in range(2)
                        for t in range(where_ref.shape[1] // TILE)
                    ],
                    axis=0,
                )
                product = dot(weights[:, :held], x_buf[row])
                beam = product[:all_beams] + sign * pltpu.roll(product[all_beams:], frames, 1)
                for to in range(line):
                    part[j, to, cc] = beam[to * beams : (to + 1) * beams]
            begin(j, at)
            return carry

        lax.fori_loop(0, gangs, chan_body, 0)

    def right_copy(j, to, g):
        return pltpu.make_async_remote_copy(
            src_ref=out_buf.at[j, to, pl.ds(g * GANG, GANG)],
            dst_ref=in_right.at[j, to, pl.ds(g * GANG, GANG)],
            send_sem=z_ss.at[j, to, g],
            recv_sem=zr_rs.at[j, to, g],
            device_id=(s, jnp.minimum(d + PAIR, doms - PAIR + y)),
            device_id_type=MESH,
        )

    def left_copy(j, to, g):
        return pltpu.make_async_remote_copy(
            src_ref=out_buf.at[j, to, pl.ds(g * GANG, GANG)],
            dst_ref=in_left.at[j, to, pl.ds(g * GANG, GANG)],
            send_sem=z_ss.at[j, to, g],
            recv_sem=zl_rs.at[j, to, g],
            device_id=(s, jnp.maximum(d - PAIR, y)),
            device_id_type=MESH,
        )

    def begin(j, g):
        span = pl.ds(g * GANG, GANG)
        for to in range(line - 1, 0, -1):

            @pl.when(z == 0)
            def _():
                out_buf[j, to, span] = part[j, to, span].astype(jnp.bfloat16)
                right_copy(j, to, g).start()

        for to in range(line - 1):

            @pl.when(z == line - 1)
            def _():
                out_buf[j, to, span] = part[j, to, span].astype(jnp.bfloat16)
                left_copy(j, to, g).start()

    def relay_right(j):
        for g in range(gangs):
            span = pl.ds(g * GANG, GANG)
            for to in range(line - 1, 0, -1):

                @pl.when(z < to)
                def _():
                    right_copy(j, to, g).wait_recv()
                    total = part[j, to, span] + in_right[j, to, span].astype(jnp.float32)
                    out_buf[j, to, span] = total.astype(jnp.bfloat16)
                    right_copy(j, to, g).start()

    def relay_left(j):
        for g in range(gangs):
            span = pl.ds(g * GANG, GANG)
            for to in range(line - 1):

                @pl.when(z > to)
                def _():
                    left_copy(j, to, g).wait_recv()
                    total = part[j, to, span] + in_left[j, to, span].astype(jnp.float32)
                    out_buf[j, to, span] = total.astype(jnp.bfloat16)
                    left_copy(j, to, g).start()

    def power_copy(j, k):
        g = (me + k) % group
        return pltpu.make_async_remote_copy(
            src_ref=pw.at[j, g],
            dst_ref=rx.at[me, j],
            send_sem=p_ss.at[j],
            recv_sem=p_rs.at[j],
            device_id=node(g),
            device_id_type=MESH,
        )

    def power_all(j):
        return pltpu.make_async_remote_copy(
            src_ref=pw.at[j, pl.ds(0, group - 1)],
            dst_ref=rx.at[pl.ds(0, group - 1), j],
            send_sem=p_ss.at[j],
            recv_sem=p_rs.at[j],
            device_id=node((me + 1) % group),
            device_id_type=MESH,
        )

    lane = lax.broadcasted_iota(jnp.int32, (1, LANES), 1)
    bins = lane % frames
    kappa = jnp.where(bins < frames // 2, bins, bins - frames).astype(jnp.float32)
    turn_rate = kappa * kappa * (0.5 / frames)
    quarter = jnp.where(first_half, 0.0, 0.25)

    def finish(j):
        sums[...] = part[j, z].reshape(count * beams, LANES)

        @pl.when(z > 0)
        def _():
            for g in range(gangs):
                right_copy(j, z, g).wait_recv()
            sums[...] += in_right[j, z].astype(jnp.float32).reshape(count * beams, LANES)

        @pl.when(z < line - 1)
        def _():
            for g in range(gangs):
                left_copy(j, z, g).wait_recv()
            sums[...] += in_left[j, z].astype(jnp.float32).reshape(count * beams, LANES)

        within = lax.broadcasted_iota(jnp.int32, (count, LANES), 0)
        chan = me * half + j * count + within
        freq = 1.0 + chan.astype(jnp.float32) * (1.0 / total)
        rate = turn_rate / (freq * freq * freq)
        rows = [sums[pl.ds(b, count, stride=beams), :] for b in range(beams)]
        x = jnp.concatenate(rows, axis=0)
        high = x.astype(jnp.bfloat16)
        low = (x - high.astype(jnp.float32)).astype(jnp.bfloat16)
        spec = dot(high, fh_ref[...]) + dot(low, fh_ref[...]) + dot(high, fl_ref[...])
        turns = jnp.concatenate([meas_ref[b : b + 1, :] * rate - quarter for b in range(beams)], axis=0)
        chirp = cos_turns(turns)
        other = pltpu.roll(chirp, frames, 1)
        cosine = jnp.where(first_half, chirp, other)
        sine = jnp.where(first_half, -other, chirp)
        turned = spec[:, :LANES] * cosine + spec[:, LANES:] * sine
        high = turned.astype(jnp.bfloat16)
        low = (turned - high.astype(jnp.float32)).astype(jnp.bfloat16)
        series = dot(high, gh_ref[...]) + dot(low, gh_ref[...]) + dot(high, gl_ref[...])
        square = series * series
        power = square + pltpu.roll(square, frames, 1)
        if pack == 2:
            power = power.reshape(beams // 2, 2, count, LANES)
            power = jnp.where(first_half[None], power[:, 0], power[:, 1])
        pw[j] = power.reshape(group, per // pack * count, LANES).astype(jnp.bfloat16)
        for k in range(1, group):
            power_copy(j, k).start()
        rx[me, j] = pw[j, me]

    channelise(0)
    for q in range(blocks):

        @pl.when(jnp.logical_not(lut_from_self(q)))
        def _():
            lut_wait(q).wait_recv()

    for q in range(blocks):
        lut[pl.ds(q * chans, chans), :] = lut_rx[q].astype(jnp.float32).reshape(LANES, chans).T

    def drain(j):
        for g in range(gangs):
            y_copy(j, g).wait_send()
        for to in range(line):

            @pl.when(z < to)
            def _():
                for g in range(gangs):
                    right_copy(j, to, g).wait_send()

            @pl.when(z > to)
            def _():
                for g in range(gangs):
                    left_copy(j, to, g).wait_send()

        power_all(j).wait()
    early = chunk_pass // 2
    late = line

    def step_body(i, carry):
        @pl.when(i < chunks)
        def _():
            form(i)

        right_at = i - z
        left_at = i - (line - 1 - z)

        @pl.when((z > 0) & (right_at >= 0) & (right_at < chunks))
        def _():
            relay_right(right_at)

        @pl.when((z < line - 1) & (left_at >= 0) & (left_at < chunks))
        def _():
            relay_left(left_at)

        @pl.when(i >= late)
        def _():
            finish(i - late)

        @pl.when(i >= late + 2)
        def _():
            drain(i - late - 2)

        return carry

    lax.fori_loop(0, early, step_body, 0)
    channelise(1)
    lax.fori_loop(early, chunks + late, step_body, 0)
    for j in range(chunks - 2, chunks):
        drain(j)

    for m in range(blocks):

        @pl.when(jnp.logical_not(lut_to_self(m)))
        def _():
            lut_copy(m).wait_send()

    result = pltpu.make_async_copy(rx, out_ref, out_sem)
    result.start()
    result.wait()


def arrange_kernel(x_ref, out_ref):
    group, chunks, rows, _ = x_ref.shape
    per, frames, _ = out_ref.shape
    pack = 2 - per % 2
    count = rows * pack // per
    half = chunks * count
    for g in range(group):
        for b in range(per // pack):
            block = x_ref[g, :, b * count : (b + 1) * count, :].reshape(half, LANES).astype(jnp.float32).T
            for part in range(pack):
                at = pl.ds(g * half, half)
                out_ref[b * pack + part, :, at] = block[part * frames : (part + 1) * frames]


def arrange(x, per, frames, total):
    vmem = pl.BlockSpec(memory_space=pltpu.VMEM)
    return pl.pallas_call(
        arrange_kernel,
        in_specs=[vmem],
        out_specs=vmem,
        out_shape=jax.ShapeDtypeStruct((per, frames, total), jnp.float32),
        name="arrange",
    )(x)


def body(voltages, station_map, beam_table, weight_table, dm_trial):
    sections = lax.axis_size("section")
    doms = lax.axis_size("dom")
    stations, frames, nfft = voltages.shape
    beams = beam_table.shape[0]
    chans = weight_table.shape[2]
    total = chans * doms
    line = doms // PAIR
    group = sections * PAIR
    per = beams // (sections * doms)
    half = total // group
    here = beams // line
    count = half // CHUNKS
    held = PAIR * stations

    table = dft_rows(nfft, total, sections, PASSES)
    matrices = frame_matrices(frames)

    vmem = pl.BlockSpec(memory_space=pltpu.VMEM)
    hbm = pl.BlockSpec(memory_space=pl.ANY)
    dma = pltpu.SemaphoreType.DMA
    bf16, f32 = jnp.bfloat16, jnp.float32
    power = pl.pallas_call(
        functools.partial(kernel, sections, doms, per, total),
        in_specs=[hbm] * 3 + [vmem, vmem, pl.BlockSpec(memory_space=pltpu.SMEM)] + [vmem] * 4,
        out_specs=hbm,
        out_shape=jax.ShapeDtypeStruct((group, CHUNKS, per * count // (2 - per % 2), LANES), bf16),
        scratch_shapes=[
            pltpu.VMEM((stations * frames, nfft), bf16),
            pltpu.VMEM(table.shape[1:], bf16),
            pltpu.VMEM((PAIR * half // PASSES * (stations + PAD), LANES), f32),
            pltpu.VMEM((CHUNKS, count, stations, LANES), bf16),
            pltpu.VMEM((half, held, LANES), bf16),
            pltpu.VMEM((CHUNKS, line, count, here, LANES), f32),
            pltpu.VMEM((CHUNKS, line, count, here, LANES), bf16),
            pltpu.VMEM((CHUNKS, line, count, here, LANES), bf16),
            pltpu.VMEM((CHUNKS, line, count, here, LANES), bf16),
            pltpu.VMEM((count * here, LANES), f32),
            pltpu.VMEM((CHUNKS, group, per * count // (2 - per % 2), LANES), bf16),
            pltpu.VMEM((group, CHUNKS, per * count // (2 - per % 2), LANES), bf16),
            pltpu.VMEM((half // chans,) + weight_table.shape, bf16),
            pltpu.VMEM((half, LANES), f32),
            pltpu.VMEM((2, beams, LANES), jnp.int16),
            pltpu.VMEM((here, LANES), f32),
            dma((stations * frames // ROWS,)),
            dma((PASSES,)),
            dma((CHUNKS, count // GANG)),
            dma((CHUNKS, count // GANG)),
            dma((CHUNKS, line, count // GANG)),
            dma((CHUNKS, line, count // GANG)),
            dma((CHUNKS, line, count // GANG)),
            dma((CHUNKS,)),
            dma((CHUNKS,)),
            dma((half // chans,)),
            dma((half // chans,)),
            dma,
            dma,
        ],
        compiler_params=pltpu.CompilerParams(
            collective_id=0, has_side_effects=True, vmem_limit_bytes=60 << 20
        ),
        cost_estimate=pl.CostEstimate(
            flops=2 * stations * frames * nfft * 2 * total // sections,
            bytes_accessed=2 * stations * frames * nfft,
            transcendentals=0,
        ),
        name="beamformer",
    )(
        voltages.reshape(stations * frames, nfft),
        jnp.asarray(table),
        weight_table,
        station_map,
        beam_table,
        dm_trial,
        *(jnp.asarray(m) for m in matrices),
    )
    return arrange(power, per, frames, total)


def solution(mesh):
    in_specs = (P("dom", None, None), P(), P(), P(None, None, "dom"), P())
    out_specs = P(("section", "dom"), None, None)
    return jax.shard_map(body, mesh=mesh, in_specs=in_specs, out_specs=out_specs, check_vma=False)
```

```python
import functools
import math

import jax
import jax.numpy as jnp
import ml_dtypes
import numpy as np
from jax import lax
from jax.experimental import pallas as pl
from jax.experimental.pallas import tpu as pltpu
from jax.sharding import PartitionSpec as P

NTAB = 64
NDM = 32
LANES = 128
TILE = 16
PAIR = 2
CHUNKS = 8
PASSES = 2
ROWS = 1024
PAD = 8
GANG = 8
MESH = pl.DeviceIdType.MESH


def dft_rows(nfft, total, sections, passes):
    section = total // sections
    half = section // PAIR
    order = np.arange(half).reshape(passes, -1)
    start = np.arange(sections)[:, None, None, None] * section
    chan = start + np.arange(PAIR)[None, None, :, None] * half + order[None, :, None, :]
    chan = chan.reshape(sections, passes, -1)
    sample = np.arange(nfft)
    window = (0.5 - 0.5 * np.cos(sample * (2.0 * math.pi / nfft))) / math.sqrt(nfft)
    angle = np.arange(nfft) * (2.0 * math.pi / nfft)
    cosine, sine = np.cos(angle), np.sin(angle)
    turn = chan[..., None] * sample % nfft
    rows = np.concatenate((cosine[turn] * window, -sine[turn] * window), axis=2)
    return rows.astype(np.float32).astype(ml_dtypes.bfloat16)


def split(values):
    values = values.astype(np.float32)
    high = values.astype(ml_dtypes.bfloat16)
    return high, (values - high.astype(np.float32)).astype(ml_dtypes.bfloat16)


def frame_matrices(frames):
    index = np.arange(frames)
    angle = (index[:, None] * index[None, :] % frames) * (2.0 * math.pi / frames)
    cosine, sine = np.cos(angle), np.sin(angle)
    real = np.concatenate((cosine, sine), axis=0)
    imag = np.concatenate((-sine, cosine), axis=0)
    forward = np.concatenate((real, imag, imag, real), axis=1)
    back_real = np.concatenate((cosine, -sine), axis=0)
    back_imag = np.concatenate((sine, cosine), axis=0)
    inverse = np.concatenate((back_real, back_imag), axis=1) / frames
    return split(forward) + split(inverse)


def pick_lanes(entries, where):
    dims = lax.GatherDimensionNumbers(
        offset_dims=(),
        collapsed_slice_dims=(1,),
        start_index_map=(1,),
        operand_batching_dims=(0,),
        start_indices_batching_dims=(0,),
    )
    return lax.gather(
        entries,
        where[..., None],
        dims,
        slice_sizes=(1, 1),
        mode=lax.GatherScatterMode.PROMISE_IN_BOUNDS,
    )


def dot(a, b):
    return jnp.dot(a, b, preferred_element_type=jnp.float32)


def cos_turns(turns):
    t = turns - jnp.round(turns)
    q = 0.25 - jnp.abs(t)
    x = q * q
    coeff = [(-1) ** k * (2.0 * math.pi) ** (2 * k + 1) / math.factorial(2 * k + 1) for k in range(7)]
    total = jnp.full_like(x, coeff[-1])
    for c in coeff[-2::-1]:
        total = total * x + c
    return total * q


def kernel(
    sections, doms, per, total,
    v_hbm, table_hbm, lut_ref, map_ref, beam_ref, trial_ref, fh_ref, fl_ref, gh_ref, gl_ref,
    out_ref,
    volts, table, lanes, ysend, x_buf, part, out_buf, in_right, in_left, sums, pw, rx, lut_rx, lut, where_ref, meas_ref,
    v_sem, t_sem, y_ss, y_rs, z_ss, zr_rs, zl_rs, p_ss, p_rs, l_ss, l_rs, l_sem, out_sem,
):
    s = lax.axis_index("section")
    d = lax.axis_index("dom")
    z = d // PAIR
    y = d % PAIR
    line = doms // PAIR
    group = sections * PAIR
    me = s * PAIR + y
    stations = ysend.shape[2]
    frames = LANES // 2
    chunks, _, count, beams, _ = part.shape
    half = chunks * count
    chans = lut_ref.shape[2]
    blocks = half // chans
    pack = 2 - per % 2
    tiles = volts.shape[0] // ROWS
    held = x_buf.shape[1]

    def load(tile):
        span = pl.ds(pl.multiple_of(tile * ROWS, ROWS), ROWS)
        return pltpu.make_async_copy(v_hbm.at[span], volts.at[span], v_sem.at[tile])

    def load_table(step):
        return pltpu.make_async_copy(table_hbm.at[s, step], table.at[step], t_sem.at[step])

    load_table(0).start()
    lax.fori_loop(0, tiles, lambda t, c: (load(t).start(), c)[1], 0)
    for step in range(1, PASSES):
        load_table(step).start()

    def node(g):
        return (g // PAIR, z * PAIR + g % PAIR)

    target_s = d // (blocks * PAIR)
    target_y = d // blocks % PAIR
    block_slot = d % blocks
    home_z = z % sections

    def lut_target(m):
        return (target_s, (m * sections + s) * PAIR + target_y)

    def lut_to_self(m):
        dev = lut_target(m)
        return (dev[0] == s) & (dev[1] == d)

    def lut_source(q):
        return (home_z, me * blocks + q)

    def lut_from_self(q):
        dev = lut_source(q)
        return (dev[0] == s) & (dev[1] == d)

    def lut_copy(m):
        return pltpu.make_async_remote_copy(
            src_ref=lut_ref,
            dst_ref=lut_rx.at[block_slot],
            send_sem=l_ss.at[m],
            recv_sem=l_rs.at[block_slot],
            device_id=lut_target(m),
            device_id_type=MESH,
        )

    def lut_wait(q):
        return pltpu.make_async_remote_copy(
            src_ref=lut_ref,
            dst_ref=lut_rx.at[q],
            send_sem=l_ss.at[0],
            recv_sem=l_rs.at[q],
            device_id=(s, d),
            device_id_type=MESH,
        )

    barrier = pltpu.get_barrier_semaphore()
    for k in range(1, group):
        pl.semaphore_signal(barrier, 1, device_id=node((me + k) % group), device_id_type=MESH)

    @pl.when(z > 0)
    def _():
        pl.semaphore_signal(barrier, 1, device_id=(s, d - PAIR), device_id_type=MESH)

    @pl.when(z < line - 1)
    def _():
        pl.semaphore_signal(barrier, 1, device_id=(s, d + PAIR), device_id_type=MESH)

    for q in range(blocks):

        @pl.when(jnp.logical_not(lut_from_self(q)))
        def _():
            pl.semaphore_signal(barrier, 1, device_id=lut_source(q), device_id_type=MESH)

    arrivals = group - 1 + (z > 0).astype(jnp.int32) + (z < line - 1).astype(jnp.int32)
    for m in range(blocks):
        arrivals = arrivals + jnp.logical_not(lut_to_self(m)).astype(jnp.int32)

    def enter():
        pl.semaphore_wait(barrier, arrivals)
        for m in range(blocks):

            @pl.when(jnp.logical_not(lut_to_self(m)))
            def _():
                lut_copy(m).start()

            @pl.when(lut_to_self(m))
            def _():
                own = pltpu.make_async_copy(lut_ref, lut_rx.at[block_slot], l_sem)
                own.start()
                own.wait()

    first_half = lax.broadcasted_iota(jnp.int32, (1, LANES), 1) < frames
    half_rows = half // PASSES * PAIR
    pitch = lanes.shape[0] // half_rows
    chunk_pass = chunks // PASSES

    gangs = count // GANG

    def y_copy(j, g):
        return pltpu.make_async_remote_copy(
            src_ref=ysend.at[j, pl.ds(g * GANG, GANG)],
            dst_ref=x_buf.at[pl.ds(j * count + g * GANG, GANG), pl.ds(pl.multiple_of(y * stations, TILE), stations)],
            send_sem=y_ss.at[j, g],
            recv_sem=y_rs.at[j, g],
            device_id=(s, z * PAIR + 1 - y),
            device_id_type=MESH,
        )

    def channelise(step):
        load_table(step).wait()

        def tile_body(tile, carry):
            if step == 0:
                load(tile).wait()
            span = pl.ds(pl.multiple_of(tile * ROWS, ROWS), ROWS)
            o = lax.dot_general(
                table[step], volts[span], (((1,), (1,)), ((), ())), preferred_element_type=jnp.float32
            )
            for two in range(ROWS // LANES):
                a = o[:half_rows, two * LANES : (two + 1) * LANES]
                b = o[half_rows:, two * LANES : (two + 1) * LANES]
                even = jnp.where(first_half, a, pltpu.roll(b, frames, 1))
                odd = jnp.where(first_half, pltpu.roll(a, frames, 1), b)
                row = tile * (ROWS // frames) + two * (LANES // frames)
                lanes[pl.ds(row, half_rows, stride=pitch), :] = even
                lanes[pl.ds(row + 1, half_rows, stride=pitch), :] = odd
            return carry

        lax.fori_loop(0, tiles, tile_body, 0)
        if step == 0:
            enter()

        def spectra(of, jj, cc):
            row = ((of * chunk_pass + jj) * count + cc) * pitch
            return lanes[pl.ds(row, stations), :].astype(jnp.bfloat16)

        def send_body(jj, carry):
            j = jj + step * chunk_pass
            for cc in range(count):
                ysend[j, cc] = spectra(1 - y, jj, cc)
                if (cc + 1) % GANG == 0:
                    y_copy(j, cc // GANG).start()
            return carry

        lax.fori_loop(0, chunk_pass, send_body, 0)

        def keep_body(jj, carry):
            j = jj + step * chunk_pass
            for cc in range(count):
                x_buf[j * count + cc, pl.ds(pl.multiple_of(y * stations, TILE), stations)] = spectra(y, jj, cc)
            return carry

        lax.fori_loop(0, chunk_pass, keep_body, 0)

    sign = jnp.where(first_half, -1.0, 1.0)

    def form(j):
        def chan_body(at, carry):
            y_copy(j, at).wait_recv()
            for step in range(GANG):
                cc = at * GANG + step
                row = j * count + cc
                entry = jnp.broadcast_to(lut[pl.ds(row, 1), :].astype(jnp.bfloat16), (TILE, LANES))
                weights = jnp.concatenate(
                    [
                        pick_lanes(entry, where_ref[p, t * TILE : (t + 1) * TILE, :])
                        for p in range(2)
                        for t in range(where_ref.shape[1] // TILE)
                    ],
                    axis=0,
                )
                product = dot(weights[:, :held], x_buf[row])
                beam = product[:all_beams] + sign * pltpu.roll(product[all_beams:], frames, 1)
                for to in range(line):
                    part[j, to, cc] = beam[to * beams : (to + 1) * beams]
            begin(j, at)
            return carry

        lax.fori_loop(0, gangs, chan_body, 0)

    def right_copy(j, to, g):
        return pltpu.make_async_remote_copy(
            src_ref=out_buf.at[j, to, pl.ds(g * GANG, GANG)],
            dst_ref=in_right.at[j, to, pl.ds(g * GANG, GANG)],
            send_sem=z_ss.at[j, to, g],
            recv_sem=zr_rs.at[j, to, g],
            device_id=(s, jnp.minimum(d + PAIR, doms - PAIR + y)),
            device_id_type=MESH,
        )

    def left_copy(j, to, g):
        return pltpu.make_async_remote_copy(
            src_ref=out_buf.at[j, to, pl.ds(g * GANG, GANG)],
            dst_ref=in_left.at[j, to, pl.ds(g * GANG, GANG)],
            send_sem=z_ss.at[j, to, g],
            recv_sem=zl_rs.at[j, to, g],
            device_id=(s, jnp.maximum(d - PAIR, y)),
            device_id_type=MESH,
        )

    def begin(j, g):
        span = pl.ds(g * GANG, GANG)
        for to in range(line - 1, 0, -1):

            @pl.when(z == 0)
            def _():
                out_buf[j, to, span] = part[j, to, span].astype(jnp.bfloat16)
                right_copy(j, to, g).start()

        for to in range(line - 1):

            @pl.when(z == line - 1)
            def _():
                out_buf[j, to, span] = part[j, to, span].astype(jnp.bfloat16)
                left_copy(j, to, g).start()

    def relay_right(j):
        for g in range(gangs):
            span = pl.ds(g * GANG, GANG)
            for to in range(line - 1, 0, -1):

                @pl.when(z < to)
                def _():
                    right_copy(j, to, g).wait_recv()
                    total = part[j, to, span] + in_right[j, to, span].astype(jnp.float32)
                    out_buf[j, to, span] = total.astype(jnp.bfloat16)
                    right_copy(j, to, g).start()

    def relay_left(j):
        for g in range(gangs):
            span = pl.ds(g * GANG, GANG)
            for to in range(line - 1):

                @pl.when(z > to)
                def _():
                    left_copy(j, to, g).wait_recv()
                    total = part[j, to, span] + in_left[j, to, span].astype(jnp.float32)
                    out_buf[j, to, span] = total.astype(jnp.bfloat16)
                    left_copy(j, to, g).start()

    def power_copy(j, k):
        g = (me + k) % group
        return pltpu.make_async_remote_copy(
            src_ref=pw.at[j, g],
            dst_ref=rx.at[me, j],
            send_sem=p_ss.at[j],
            recv_sem=p_rs.at[j],
            device_id=node(g),
            device_id_type=MESH,
        )

    def power_all(j):
        return pltpu.make_async_remote_copy(
            src_ref=pw.at[j, pl.ds(0, group - 1)],
            dst_ref=rx.at[pl.ds(0, group - 1), j],
            send_sem=p_ss.at[j],
            recv_sem=p_rs.at[j],
            device_id=node((me + 1) % group),
            device_id_type=MESH,
        )

    lane = lax.broadcasted_iota(jnp.int32, (1, LANES), 1)
    bins = lane % frames
    kappa = jnp.where(bins < frames // 2, bins, bins - frames).astype(jnp.float32)
    turn_rate = kappa * kappa * (0.5 / frames)
    quarter = jnp.where(first_half, 0.0, 0.25)

    def finish(j):
        within = lax.broadcasted_iota(jnp.int32, (count, LANES), 0)
        chan = me * half + j * count + within
        freq = 1.0 + chan.astype(jnp.float32) * (1.0 / total)
        rate = turn_rate / (freq * freq * freq)
        turns = jnp.concatenate([meas_ref[b : b + 1, :] * rate - quarter for b in range(beams)], axis=0)
        chirp = cos_turns(turns)
        other = pltpu.roll(chirp, frames, 1)
        cosine = jnp.where(first_half, chirp, other)
        sine = jnp.where(first_half, -other, chirp)
        sums[...] = part[j, z].reshape(count * beams, LANES)

        @pl.when(z > 0)
        def _():
            for g in range(gangs):
                right_copy(j, z, g).wait_recv()
            sums[...] += in_right[j, z].astype(jnp.float32).reshape(count * beams, LANES)

        @pl.when(z < line - 1)
        def _():
            for g in range(gangs):
                left_copy(j, z, g).wait_recv()
            sums[...] += in_left[j, z].astype(jnp.float32).reshape(count * beams, LANES)

        rows = [sums[pl.ds(b, count, stride=beams), :] for b in range(beams)]
        x = jnp.concatenate(rows, axis=0)
        high = x.astype(jnp.bfloat16)
        low = (x - high.astype(jnp.float32)).astype(jnp.bfloat16)
        spec = dot(high, fh_ref[...]) + dot(low, fh_ref[...]) + dot(high, fl_ref[...])
        turned = spec[:, :LANES] * cosine + spec[:, LANES:] * sine
        high = turned.astype(jnp.bfloat16)
        low = (turned - high.astype(jnp.float32)).astype(jnp.bfloat16)
        series = dot(high, gh_ref[...]) + dot(low, gh_ref[...]) + dot(high, gl_ref[...])
        square = series * series
        power = square + pltpu.roll(square, frames, 1)
        if pack == 2:
            power = power.reshape(beams // 2, 2, count, LANES)
            power = jnp.where(first_half[None], power[:, 0], power[:, 1])
        pw[j] = power.reshape(group, per // pack * count, LANES).astype(jnp.bfloat16)
        for k in range(1, group):
            power_copy(j, k).start()
        rx[me, j] = pw[j, me]

    channelise(0)
    all_beams, everyone = beam_ref.shape
    stops = sections * line
    team = all_beams // stops
    row = map_ref[pl.ds(pl.multiple_of(z * held // LANES * LANES, LANES), LANES)].reshape(1, LANES)
    if held < LANES:
        row = pltpu.roll(jnp.broadcast_to(row, (8, LANES)), (LANES - z * held % LANES) % LANES, 1)[:1]
    here = (lax.broadcasted_iota(jnp.int32, (everyone, LANES), 0) == row).astype(jnp.float32)
    found = dot(beam_ref[...].astype(jnp.float32).astype(jnp.bfloat16), here.astype(jnp.bfloat16))
    ordered = [
        found[(at * line + to) * team : (at * line + to + 1) * team] for to in range(line) for at in range(sections)
    ]
    ordered = jnp.concatenate(ordered, axis=0).astype(jnp.int32)
    for part_at in range(2):
        where_ref[part_at] = (ordered + part_at * NTAB).astype(jnp.int16)
    for b in range(beams):
        trial = trial_ref[(b // team * line + z) * team + b % team]
        meas_ref[pl.ds(b, 1), :] = jnp.full((1, LANES), (trial + 1).astype(jnp.float32) * (1.0 / NDM), jnp.float32)
    for q in range(blocks):

        @pl.when(jnp.logical_not(lut_from_self(q)))
        def _():
            lut_wait(q).wait_recv()

    for q in range(blocks):
        lut[pl.ds(q * chans, chans), :] = lut_rx[q].astype(jnp.float32).reshape(LANES, chans).T

    def drain(j):
        for g in range(gangs):
            y_copy(j, g).wait_send()
        for to in range(line):

            @pl.when(z < to)
            def _():
                for g in range(gangs):
                    right_copy(j, to, g).wait_send()

            @pl.when(z > to)
            def _():
                for g in range(gangs):
                    left_copy(j, to, g).wait_send()

        power_all(j).wait()
    early = chunk_pass // 2
    late = line - 1

    def step_body(i, carry):
        right_at = i - z
        left_at = i - (line - 1 - z)

        @pl.when((z > 0) & (right_at >= 0) & (right_at < chunks))
        def _():
            relay_right(right_at)

        @pl.when((z < line - 1) & (left_at >= 0) & (left_at < chunks))
        def _():
            relay_left(left_at)

        @pl.when(i >= late)
        def _():
            finish(i - late)

        @pl.when(i < chunks)
        def _():
            form(i)

        @pl.when(i >= late + 2)
        def _():
            drain(i - late - 2)

        return carry

    lax.fori_loop(0, early, step_body, 0)
    channelise(1)
    lax.fori_loop(early, chunks + late, step_body, 0)
    for j in range(chunks - 2, chunks):
        drain(j)

    for m in range(blocks):

        @pl.when(jnp.logical_not(lut_to_self(m)))
        def _():
            lut_copy(m).wait_send()

    result = pltpu.make_async_copy(rx, out_ref, out_sem)
    result.start()
    result.wait()


def arrange_kernel(x_ref, out_ref):
    group, chunks, rows, _ = x_ref.shape
    per, frames, _ = out_ref.shape
    pack = 2 - per % 2
    count = rows * pack // per
    half = chunks * count
    for g in range(group):
        for b in range(per // pack):
            block = x_ref[g, :, b * count : (b + 1) * count, :].reshape(half, LANES).astype(jnp.float32).T
            for part in range(pack):
                at = pl.ds(g * half, half)
                out_ref[b * pack + part, :, at] = block[part * frames : (part + 1) * frames]


def arrange(x, per, frames, total):
    group, chunks, rows, _ = x.shape
    steps = 2
    return pl.pallas_call(
        arrange_kernel,
        grid=(steps,),
        in_specs=[pl.BlockSpec((group // steps, chunks, rows, LANES), lambda i: (i, 0, 0, 0))],
        out_specs=pl.BlockSpec((per, frames, total // steps), lambda i: (0, 0, i)),
        out_shape=jax.ShapeDtypeStruct((per, frames, total), jnp.float32),
        name="arrange",
    )(x)


def body(voltages, station_map, beam_table, weight_table, dm_trial):
    sections = lax.axis_size("section")
    doms = lax.axis_size("dom")
    stations, frames, nfft = voltages.shape
    beams = beam_table.shape[0]
    chans = weight_table.shape[2]
    total = chans * doms
    line = doms // PAIR
    group = sections * PAIR
    per = beams // (sections * doms)
    half = total // group
    here = beams // line
    count = half // CHUNKS
    held = PAIR * stations

    table = dft_rows(nfft, total, sections, PASSES)
    matrices = frame_matrices(frames)

    vmem = pl.BlockSpec(memory_space=pltpu.VMEM)
    hbm = pl.BlockSpec(memory_space=pl.ANY)
    dma = pltpu.SemaphoreType.DMA
    bf16, f32 = jnp.bfloat16, jnp.float32
    power = pl.pallas_call(
        functools.partial(kernel, sections, doms, per, total),
        in_specs=[hbm] * 3 + [vmem, vmem, pl.BlockSpec(memory_space=pltpu.SMEM)] + [vmem] * 4,
        out_specs=hbm,
        out_shape=jax.ShapeDtypeStruct((group, CHUNKS, per * count // (2 - per % 2), LANES), bf16),
        scratch_shapes=[
            pltpu.VMEM((stations * frames, nfft), bf16),
            pltpu.VMEM(table.shape[1:], bf16),
            pltpu.VMEM((PAIR * half // PASSES * (stations + PAD), LANES), f32),
            pltpu.VMEM((CHUNKS, count, stations, LANES), bf16),
            pltpu.VMEM((half, held, LANES), bf16),
            pltpu.VMEM((CHUNKS, line, count, here, LANES), f32),
            pltpu.VMEM((CHUNKS, line, count, here, LANES), bf16),
            pltpu.VMEM((CHUNKS, line, count, here, LANES), bf16),
            pltpu.VMEM((CHUNKS, line, count, here, LANES), bf16),
            pltpu.VMEM((count * here, LANES), f32),
            pltpu.VMEM((CHUNKS, group, per * count // (2 - per % 2), LANES), bf16),
            pltpu.VMEM((group, CHUNKS, per * count // (2 - per % 2), LANES), bf16),
            pltpu.VMEM((half // chans,) + weight_table.shape, bf16),
            pltpu.VMEM((half, LANES), f32),
            pltpu.VMEM((2, beams, LANES), jnp.int16),
            pltpu.VMEM((here, LANES), f32),
            dma((stations * frames // ROWS,)),
            dma((PASSES,)),
            dma((CHUNKS, count // GANG)),
            dma((CHUNKS, count // GANG)),
            dma((CHUNKS, line, count // GANG)),
            dma((CHUNKS, line, count // GANG)),
            dma((CHUNKS, line, count // GANG)),
            dma((CHUNKS,)),
            dma((CHUNKS,)),
            dma((half // chans,)),
            dma((half // chans,)),
            dma,
            dma,
        ],
        compiler_params=pltpu.CompilerParams(
            collective_id=0, has_side_effects=True, vmem_limit_bytes=60 << 20
        ),
        cost_estimate=pl.CostEstimate(
            flops=2 * stations * frames * nfft * 2 * total // sections,
            bytes_accessed=2 * stations * frames * nfft,
            transcendentals=0,
        ),
        name="beamformer",
    )(
        voltages.reshape(stations * frames, nfft),
        jnp.asarray(table),
        weight_table,
        station_map,
        beam_table,
        dm_trial,
        *(jnp.asarray(m) for m in matrices),
    )
    return arrange(power, per, frames, total)


def solution(mesh):
    in_specs = (P("dom", None, None), P(), P(), P(None, None, "dom"), P())
    out_specs = P(("section", "dom"), None, None)
    return jax.shard_map(body, mesh=mesh, in_specs=in_specs, out_specs=out_specs, check_vma=False)
```

```python
import functools
import math

import jax
import jax.numpy as jnp
import ml_dtypes
import numpy as np
from jax import lax
from jax.experimental import pallas as pl
from jax.experimental.pallas import tpu as pltpu
from jax.sharding import PartitionSpec as P

NTAB = 64
NDM = 32
LANES = 128
TILE = 16
PAIR = 2
CHUNKS = 8
PASSES = 2
ROWS = 1024
PAD = 8
GANG = 8
MESH = pl.DeviceIdType.MESH


def dft_rows(nfft, total, sections, passes):
    section = total // sections
    half = section // PAIR
    order = np.arange(half).reshape(passes, -1)
    start = np.arange(sections)[:, None, None, None] * section
    chan = start + np.arange(PAIR)[None, None, :, None] * half + order[None, :, None, :]
    chan = chan.reshape(sections, passes, -1)
    sample = np.arange(nfft)
    window = (0.5 - 0.5 * np.cos(sample * (2.0 * math.pi / nfft))) / math.sqrt(nfft)
    angle = np.arange(nfft) * (2.0 * math.pi / nfft)
    cosine, sine = np.cos(angle), np.sin(angle)
    turn = chan[..., None] * sample % nfft
    rows = np.concatenate((cosine[turn] * window, -sine[turn] * window), axis=2)
    return rows.astype(np.float32).astype(ml_dtypes.bfloat16)


def split(values):
    values = values.astype(np.float32)
    high = values.astype(ml_dtypes.bfloat16)
    return high, (values - high.astype(np.float32)).astype(ml_dtypes.bfloat16)


def frame_matrices(frames):
    index = np.arange(frames)
    angle = (index[:, None] * index[None, :] % frames) * (2.0 * math.pi / frames)
    cosine, sine = np.cos(angle), np.sin(angle)
    real = np.concatenate((cosine, sine), axis=0)
    imag = np.concatenate((-sine, cosine), axis=0)
    forward = np.concatenate((real, imag, imag, real), axis=1)
    back_real = np.concatenate((cosine, -sine), axis=0)
    back_imag = np.concatenate((sine, cosine), axis=0)
    inverse = np.concatenate((back_real, back_imag), axis=1) / frames
    return split(forward) + split(inverse)


def pick_lanes(entries, where):
    dims = lax.GatherDimensionNumbers(
        offset_dims=(),
        collapsed_slice_dims=(1,),
        start_index_map=(1,),
        operand_batching_dims=(0,),
        start_indices_batching_dims=(0,),
    )
    return lax.gather(
        entries,
        where[..., None],
        dims,
        slice_sizes=(1, 1),
        mode=lax.GatherScatterMode.PROMISE_IN_BOUNDS,
    )


def dot(a, b):
    return jnp.dot(a, b, preferred_element_type=jnp.float32)


def cos_turns(turns):
    t = turns - jnp.round(turns)
    q = 0.25 - jnp.abs(t)
    x = q * q
    coeff = [(-1) ** k * (2.0 * math.pi) ** (2 * k + 1) / math.factorial(2 * k + 1) for k in range(7)]
    total = jnp.full_like(x, coeff[-1])
    for c in coeff[-2::-1]:
        total = total * x + c
    return total * q


def kernel(
    sections, doms, per, total,
    v_hbm, table_hbm, lut_ref, map_ref, beam_ref, trial_ref, fh_ref, fl_ref, gh_ref, gl_ref,
    out_ref,
    volts, table, lanes, ysend, x_buf, part, out_buf, in_right, in_left, sums, pw, rx, lut_rx, lut, where_ref, meas_ref,
    v_sem, t_sem, y_ss, y_rs, z_ss, zr_rs, zl_rs, p_ss, p_rs, l_ss, l_rs, l_sem, out_sem,
):
    s = lax.axis_index("section")
    d = lax.axis_index("dom")
    z = d // PAIR
    y = d % PAIR
    line = doms // PAIR
    group = sections * PAIR
    me = s * PAIR + y
    stations = ysend.shape[2]
    frames = LANES // 2
    chunks, _, count, beams, _ = part.shape
    half = chunks * count
    chans = lut_ref.shape[2]
    blocks = half // chans
    pack = 2 - per % 2
    tiles = volts.shape[0] // ROWS
    held = x_buf.shape[1]

    def load(tile):
        span = pl.ds(pl.multiple_of(tile * ROWS, ROWS), ROWS)
        return pltpu.make_async_copy(v_hbm.at[span], volts.at[span], v_sem.at[tile])

    def load_table(step):
        return pltpu.make_async_copy(table_hbm.at[s, step], table.at[step], t_sem.at[step])

    load_table(0).start()
    lax.fori_loop(0, tiles, lambda t, c: (load(t).start(), c)[1], 0)
    for step in range(1, PASSES):
        load_table(step).start()

    def node(g):
        return (g // PAIR, z * PAIR + g % PAIR)

    target_s = d // (blocks * PAIR)
    target_y = d // blocks % PAIR
    block_slot = d % blocks
    home_z = z % sections

    def lut_target(m):
        return (target_s, (m * sections + s) * PAIR + target_y)

    def lut_to_self(m):
        dev = lut_target(m)
        return (dev[0] == s) & (dev[1] == d)

    def lut_source(q):
        return (home_z, me * blocks + q)

    def lut_from_self(q):
        dev = lut_source(q)
        return (dev[0] == s) & (dev[1] == d)

    def lut_copy(m):
        return pltpu.make_async_remote_copy(
            src_ref=lut_ref,
            dst_ref=lut_rx.at[block_slot],
            send_sem=l_ss.at[m],
            recv_sem=l_rs.at[block_slot],
            device_id=lut_target(m),
            device_id_type=MESH,
        )

    def lut_wait(q):
        return pltpu.make_async_remote_copy(
            src_ref=lut_ref,
            dst_ref=lut_rx.at[q],
            send_sem=l_ss.at[0],
            recv_sem=l_rs.at[q],
            device_id=(s, d),
            device_id_type=MESH,
        )

    barrier = pltpu.get_barrier_semaphore()
    for k in range(1, group):
        pl.semaphore_signal(barrier, 1, device_id=node((me + k) % group), device_id_type=MESH)

    @pl.when(z > 0)
    def _():
        pl.semaphore_signal(barrier, 1, device_id=(s, d - PAIR), device_id_type=MESH)

    @pl.when(z < line - 1)
    def _():
        pl.semaphore_signal(barrier, 1, device_id=(s, d + PAIR), device_id_type=MESH)

    for q in range(blocks):

        @pl.when(jnp.logical_not(lut_from_self(q)))
        def _():
            pl.semaphore_signal(barrier, 1, device_id=lut_source(q), device_id_type=MESH)

    arrivals = group - 1 + (z > 0).astype(jnp.int32) + (z < line - 1).astype(jnp.int32)
    for m in range(blocks):
        arrivals = arrivals + jnp.logical_not(lut_to_self(m)).astype(jnp.int32)

    def enter():
        pl.semaphore_wait(barrier, arrivals)
        for m in range(blocks):

            @pl.when(jnp.logical_not(lut_to_self(m)))
            def _():
                lut_copy(m).start()

            @pl.when(lut_to_self(m))
            def _():
                own = pltpu.make_async_copy(lut_ref, lut_rx.at[block_slot], l_sem)
                own.start()
                own.wait()

    first_half = lax.broadcasted_iota(jnp.int32, (1, LANES), 1) < frames
    half_rows = half // PASSES * PAIR
    pitch = lanes.shape[0] // half_rows
    chunk_pass = chunks // PASSES

    gangs = count // GANG

    def y_copy(j, g):
        return pltpu.make_async_remote_copy(
            src_ref=ysend.at[j, pl.ds(g * GANG, GANG)],
            dst_ref=x_buf.at[pl.ds(j * count + g * GANG, GANG), pl.ds(pl.multiple_of(y * stations, TILE), stations)],
            send_sem=y_ss.at[j, g],
            recv_sem=y_rs.at[j, g],
            device_id=(s, z * PAIR + 1 - y),
            device_id_type=MESH,
        )

    def channelise(step):
        load_table(step).wait()

        def tile_body(tile, carry):
            if step == 0:
                load(tile).wait()
            span = pl.ds(pl.multiple_of(tile * ROWS, ROWS), ROWS)
            o = lax.dot_general(
                table[step], volts[span], (((1,), (1,)), ((), ())), preferred_element_type=jnp.float32
            )
            for two in range(ROWS // LANES):
                a = o[:half_rows, two * LANES : (two + 1) * LANES]
                b = o[half_rows:, two * LANES : (two + 1) * LANES]
                even = jnp.where(first_half, a, pltpu.roll(b, frames, 1))
                odd = jnp.where(first_half, pltpu.roll(a, frames, 1), b)
                row = tile * (ROWS // frames) + two * (LANES // frames)
                lanes[pl.ds(row, half_rows, stride=pitch), :] = even
                lanes[pl.ds(row + 1, half_rows, stride=pitch), :] = odd
            return carry

        lax.fori_loop(0, tiles, tile_body, 0)
        if step == 0:
            enter()

        def spectra(of, jj, cc):
            row = ((of * chunk_pass + jj) * count + cc) * pitch
            return lanes[pl.ds(row, stations), :].astype(jnp.bfloat16)

        def send_body(jj, carry):
            j = jj + step * chunk_pass
            for cc in range(count):
                ysend[j, cc] = spectra(1 - y, jj, cc)
                if (cc + 1) % GANG == 0:
                    y_copy(j, cc // GANG).start()
            return carry

        lax.fori_loop(0, chunk_pass, send_body, 0)

        def keep_body(jj, carry):
            j = jj + step * chunk_pass
            for cc in range(count):
                x_buf[j * count + cc, pl.ds(pl.multiple_of(y * stations, TILE), stations)] = spectra(y, jj, cc)
            return carry

        lax.fori_loop(0, chunk_pass, keep_body, 0)

    sign = jnp.where(first_half, -1.0, 1.0)

    def form(j):
        def chan_body(at, carry):
            y_copy(j, at).wait_recv()
            for step in range(GANG):
                cc = at * GANG + step
                row = j * count + cc
                entry = jnp.broadcast_to(lut[pl.ds(row, 1), :].astype(jnp.bfloat16), (TILE, LANES))
                weights = jnp.concatenate(
                    [
                        pick_lanes(entry, where_ref[p, t * TILE : (t + 1) * TILE, :])
                        for p in range(2)
                        for t in range(where_ref.shape[1] // TILE)
                    ],
                    axis=0,
                )
                product = dot(weights[:, :held], x_buf[row])
                beam = product[:all_beams] + sign * pltpu.roll(product[all_beams:], frames, 1)
                for to in range(line):
                    part[j, to, cc] = beam[to * beams : (to + 1) * beams]
            begin(j, at)
            return carry

        lax.fori_loop(0, gangs, chan_body, 0)

    def right_copy(j, to, g):
        return pltpu.make_async_remote_copy(
            src_ref=out_buf.at[j, to, pl.ds(g * GANG, GANG)],
            dst_ref=in_right.at[j, to, pl.ds(g * GANG, GANG)],
            send_sem=z_ss.at[j, to, g],
            recv_sem=zr_rs.at[j, to, g],
            device_id=(s, jnp.minimum(d + PAIR, doms - PAIR + y)),
            device_id_type=MESH,
        )

    def left_copy(j, to, g):
        return pltpu.make_async_remote_copy(
            src_ref=out_buf.at[j, to, pl.ds(g * GANG, GANG)],
            dst_ref=in_left.at[j, to, pl.ds(g * GANG, GANG)],
            send_sem=z_ss.at[j, to, g],
            recv_sem=zl_rs.at[j, to, g],
            device_id=(s, jnp.maximum(d - PAIR, y)),
            device_id_type=MESH,
        )

    def begin(j, g):
        span = pl.ds(g * GANG, GANG)
        for to in range(line - 1, 0, -1):

            @pl.when(z == 0)
            def _():
                out_buf[j, to, span] = part[j, to, span].astype(jnp.bfloat16)
                right_copy(j, to, g).start()

        for to in range(line - 1):

            @pl.when(z == line - 1)
            def _():
                out_buf[j, to, span] = part[j, to, span].astype(jnp.bfloat16)
                left_copy(j, to, g).start()

    def relay_right(j):
        for g in range(gangs):
            span = pl.ds(g * GANG, GANG)
            for to in range(line - 1, 0, -1):

                @pl.when(z < to)
                def _():
                    right_copy(j, to, g).wait_recv()
                    total = part[j, to, span] + in_right[j, to, span].astype(jnp.float32)
                    out_buf[j, to, span] = total.astype(jnp.bfloat16)
                    right_copy(j, to, g).start()

    def relay_left(j):
        for g in range(gangs):
            span = pl.ds(g * GANG, GANG)
            for to in range(line - 1):

                @pl.when(z > to)
                def _():
                    left_copy(j, to, g).wait_recv()
                    total = part[j, to, span] + in_left[j, to, span].astype(jnp.float32)
                    out_buf[j, to, span] = total.astype(jnp.bfloat16)
                    left_copy(j, to, g).start()

    def power_copy(j, k):
        g = (me + k) % group
        return pltpu.make_async_remote_copy(
            src_ref=pw.at[j, g],
            dst_ref=rx.at[me, j],
            send_sem=p_ss.at[j],
            recv_sem=p_rs.at[j],
            device_id=node(g),
            device_id_type=MESH,
        )

    def power_all(j):
        return pltpu.make_async_remote_copy(
            src_ref=pw.at[j, pl.ds(0, group - 1)],
            dst_ref=rx.at[pl.ds(0, group - 1), j],
            send_sem=p_ss.at[j],
            recv_sem=p_rs.at[j],
            device_id=node((me + 1) % group),
            device_id_type=MESH,
        )

    lane = lax.broadcasted_iota(jnp.int32, (1, LANES), 1)
    bins = lane % frames
    kappa = jnp.where(bins < frames // 2, bins, bins - frames).astype(jnp.float32)
    turn_rate = kappa * kappa * (0.5 / frames)
    quarter = jnp.where(first_half, 0.0, 0.25)

    def finish(j):
        within = lax.broadcasted_iota(jnp.int32, (count, LANES), 0)
        chan = me * half + j * count + within
        freq = 1.0 + chan.astype(jnp.float32) * (1.0 / total)
        rate = turn_rate / (freq * freq * freq)
        turns = jnp.concatenate([meas_ref[b : b + 1, :] * rate - quarter for b in range(beams)], axis=0)
        chirp = cos_turns(turns)
        other = pltpu.roll(chirp, frames, 1)
        cosine = jnp.where(first_half, chirp, other)
        sine = jnp.where(first_half, -other, chirp)
        sums[...] = part[j, z].reshape(count * beams, LANES)

        @pl.when(z > 0)
        def _():
            for g in range(gangs):
                right_copy(j, z, g).wait_recv()
            sums[...] += in_right[j, z].astype(jnp.float32).reshape(count * beams, LANES)

        @pl.when(z < line - 1)
        def _():
            for g in range(gangs):
                left_copy(j, z, g).wait_recv()
            sums[...] += in_left[j, z].astype(jnp.float32).reshape(count * beams, LANES)

        rows = [sums[pl.ds(b, count, stride=beams), :] for b in range(beams)]
        x = jnp.concatenate(rows, axis=0)
        high = x.astype(jnp.bfloat16)
        low = (x - high.astype(jnp.float32)).astype(jnp.bfloat16)
        spec = dot(high, fh_ref[...]) + dot(low, fh_ref[...]) + dot(high, fl_ref[...])
        turned = spec[:, :LANES] * cosine + spec[:, LANES:] * sine
        high = turned.astype(jnp.bfloat16)
        low = (turned - high.astype(jnp.float32)).astype(jnp.bfloat16)
        series = dot(high, gh_ref[...]) + dot(low, gh_ref[...]) + dot(high, gl_ref[...])
        square = series * series
        power = square + pltpu.roll(square, frames, 1)
        if pack == 2:
            power = power.reshape(beams // 2, 2, count, LANES)
            power = jnp.where(first_half[None], power[:, 0], power[:, 1])
        pw[j] = power.reshape(group, per // pack * count, LANES).astype(jnp.bfloat16)
        for k in range(1, group):
            power_copy(j, k).start()
        rx[me, j] = pw[j, me]

    channelise(0)
    all_beams, everyone = beam_ref.shape
    stops = sections * line
    team = all_beams // stops
    row = map_ref[pl.ds(pl.multiple_of(z * held // LANES * LANES, LANES), LANES)].reshape(1, LANES)
    if held < LANES:
        row = pltpu.roll(jnp.broadcast_to(row, (8, LANES)), (LANES - z * held % LANES) % LANES, 1)[:1]
    here = (lax.broadcasted_iota(jnp.int32, (everyone, LANES), 0) == row).astype(jnp.float32)
    found = dot(beam_ref[...].astype(jnp.float32).astype(jnp.bfloat16), here.astype(jnp.bfloat16))
    ordered = [
        found[(at * line + to) * team : (at * line + to + 1) * team] for to in range(line) for at in range(sections)
    ]
    ordered = jnp.concatenate(ordered, axis=0).astype(jnp.int32)
    for part_at in range(2):
        where_ref[part_at] = (ordered + part_at * NTAB).astype(jnp.int16)
    for b in range(beams):
        trial = trial_ref[(b // team * line + z) * team + b % team]
        meas_ref[pl.ds(b, 1), :] = jnp.full((1, LANES), (trial + 1).astype(jnp.float32) * (1.0 / NDM), jnp.float32)
    for q in range(blocks):

        @pl.when(jnp.logical_not(lut_from_self(q)))
        def _():
            lut_wait(q).wait_recv()

    for q in range(blocks):
        lut[pl.ds(q * chans, chans), :] = lut_rx[q].astype(jnp.float32).reshape(LANES, chans).T

    def drain(j):
        for g in range(gangs):
            y_copy(j, g).wait_send()
        for to in range(line):

            @pl.when(z < to)
            def _():
                for g in range(gangs):
                    right_copy(j, to, g).wait_send()

            @pl.when(z > to)
            def _():
                for g in range(gangs):
                    left_copy(j, to, g).wait_send()

    early = chunk_pass // 2
    late = line - 1

    def step_body(i, carry):
        right_at = i - z
        left_at = i - (line - 1 - z)

        @pl.when((z > 0) & (right_at >= 0) & (right_at < chunks))
        def _():
            relay_right(right_at)

        @pl.when((z < line - 1) & (left_at >= 0) & (left_at < chunks))
        def _():
            relay_left(left_at)

        @pl.when(i >= late)
        def _():
            finish(i - late)

        @pl.when(i < chunks)
        def _():
            form(i)

        @pl.when(i >= late + 2)
        def _():
            drain(i - late - 2)
            power_all(i - late - 2).wait()

        return carry

    lax.fori_loop(0, early, step_body, 0)
    channelise(1)
    lax.fori_loop(early, chunks + late, step_body, 0)
    for j in range(chunks - 2, chunks):
        power_all(j).wait_recv()
    result = pltpu.make_async_copy(rx, out_ref, out_sem)
    result.start()
    for j in range(chunks - 2, chunks):
        drain(j)
        power_all(j).wait_send()

    for m in range(blocks):

        @pl.when(jnp.logical_not(lut_to_self(m)))
        def _():
            lut_copy(m).wait_send()

    result.wait()


def arrange_kernel(x_ref, out_ref):
    group, chunks, rows, _ = x_ref.shape
    per, frames, _ = out_ref.shape
    pack = 2 - per % 2
    count = rows * pack // per
    half = chunks * count
    for g in range(group):
        for b in range(per // pack):
            block = x_ref[g, :, b * count : (b + 1) * count, :].reshape(half, LANES).astype(jnp.float32).T
            for part in range(pack):
                at = pl.ds(g * half, half)
                out_ref[b * pack + part, :, at] = block[part * frames : (part + 1) * frames]


def arrange(x, per, frames, total):
    group, chunks, rows, _ = x.shape
    steps = 2
    return pl.pallas_call(
        arrange_kernel,
        grid=(steps,),
        in_specs=[pl.BlockSpec((group // steps, chunks, rows, LANES), lambda i: (i, 0, 0, 0))],
        out_specs=pl.BlockSpec((per, frames, total // steps), lambda i: (0, 0, i)),
        out_shape=jax.ShapeDtypeStruct((per, frames, total), jnp.float32),
        name="arrange",
    )(x)


def body(voltages, station_map, beam_table, weight_table, dm_trial):
    sections = lax.axis_size("section")
    doms = lax.axis_size("dom")
    stations, frames, nfft = voltages.shape
    beams = beam_table.shape[0]
    chans = weight_table.shape[2]
    total = chans * doms
    line = doms // PAIR
    group = sections * PAIR
    per = beams // (sections * doms)
    half = total // group
    here = beams // line
    count = half // CHUNKS
    held = PAIR * stations

    table = dft_rows(nfft, total, sections, PASSES)
    matrices = frame_matrices(frames)

    vmem = pl.BlockSpec(memory_space=pltpu.VMEM)
    hbm = pl.BlockSpec(memory_space=pl.ANY)
    dma = pltpu.SemaphoreType.DMA
    bf16, f32 = jnp.bfloat16, jnp.float32
    power = pl.pallas_call(
        functools.partial(kernel, sections, doms, per, total),
        in_specs=[hbm] * 3 + [vmem, vmem, pl.BlockSpec(memory_space=pltpu.SMEM)] + [vmem] * 4,
        out_specs=hbm,
        out_shape=jax.ShapeDtypeStruct((group, CHUNKS, per * count // (2 - per % 2), LANES), bf16),
        scratch_shapes=[
            pltpu.VMEM((stations * frames, nfft), bf16),
            pltpu.VMEM(table.shape[1:], bf16),
            pltpu.VMEM((PAIR * half // PASSES * (stations + PAD), LANES), f32),
            pltpu.VMEM((CHUNKS, count, stations, LANES), bf16),
            pltpu.VMEM((half, held, LANES), bf16),
            pltpu.VMEM((CHUNKS, line, count, here, LANES), f32),
            pltpu.VMEM((CHUNKS, line, count, here, LANES), bf16),
            pltpu.VMEM((CHUNKS, line, count, here, LANES), bf16),
            pltpu.VMEM((CHUNKS, line, count, here, LANES), bf16),
            pltpu.VMEM((count * here, LANES), f32),
            pltpu.VMEM((CHUNKS, group, per * count // (2 - per % 2), LANES), bf16),
            pltpu.VMEM((group, CHUNKS, per * count // (2 - per % 2), LANES), bf16),
            pltpu.VMEM((half // chans,) + weight_table.shape, bf16),
            pltpu.VMEM((half, LANES), f32),
            pltpu.VMEM((2, beams, LANES), jnp.int16),
            pltpu.VMEM((here, LANES), f32),
            dma((stations * frames // ROWS,)),
            dma((PASSES,)),
            dma((CHUNKS, count // GANG)),
            dma((CHUNKS, count // GANG)),
            dma((CHUNKS, line, count // GANG)),
            dma((CHUNKS, line, count // GANG)),
            dma((CHUNKS, line, count // GANG)),
            dma((CHUNKS,)),
            dma((CHUNKS,)),
            dma((half // chans,)),
            dma((half // chans,)),
            dma,
            dma,
        ],
        compiler_params=pltpu.CompilerParams(
            collective_id=0, has_side_effects=True, vmem_limit_bytes=60 << 20
        ),
        cost_estimate=pl.CostEstimate(
            flops=2 * stations * frames * nfft * 2 * total // sections,
            bytes_accessed=2 * stations * frames * nfft,
            transcendentals=0,
        ),
        name="beamformer",
    )(
        voltages.reshape(stations * frames, nfft),
        jnp.asarray(table),
        weight_table,
        station_map,
        beam_table,
        dm_trial,
        *(jnp.asarray(m) for m in matrices),
    )
    return arrange(power, per, frames, total)


def solution(mesh):
    in_specs = (P("dom", None, None), P(), P(), P(None, None, "dom"), P())
    out_specs = P(("section", "dom"), None, None)
    return jax.shard_map(body, mesh=mesh, in_specs=in_specs, out_specs=out_specs, check_vma=False)
```
